512 devices in a mesh: tgt: 64 (over z, y_hi, core), sup: 8 (over x, y_lo).
Axes of the slice: x: 4, y: 8 (y_hi: 4, y_lo: 2; y = y_hi * 2 + y_lo), z: 8, core: 2. Of those that a mesh axis runs over, the one named last changes fastest.
Arguments:
- targets: float32 [512, 3, 1024], P('tgt'), may hold values from -4 to 4
- labels: int32 [512], P('tgt'), may hold values from 0 to 99
- support_slots: float32 [64, 64, 3, 1024], P('tgt', 'sup'), may hold values from -4 to 4
- block_owner: int32 [4], replicated, may hold values from 0 to 63, as said below
- dual_coeffs: float32 [4, 64, 100], P(None, 'sup'), may hold values from -0.15 to 0.15
Outputs:
- predictions: float32 [512, 100], P('tgt')
- support_grad: float32 [4, 64, 3, 1024], P(None, 'sup')
The draws below stay inside these ranges and needn't reach their ends.
Inputs may be any that keep to these rules, and one draw needn't show every extreme that they name: 4 distinct slot indices, among them 0 and 63; block b is support_slots[block_owner[b]], and the other slots are never read.
All inputs are finite; a program needn't handle non-finite values.
Results may differ from the reference program's by a relative error of at most 0.0001.
Values sent between devices are 32-bit elements; how exact they have to be, the bound alone decides.
No kernel may reach another device: no remote copies, remote signals or barrier semaphores. Data moves between devices by JAX's collectives and lax.ppermute only.
A program may use at most 64 MiB of HBM per device.

```python
import jax
import jax.numpy as jnp
from jax import lax

SIDE = 32
CH = 3
CLASSES = 100
LAYERS = 3
BLOCKS = 4
SB = 64
TGT_DEV = 8
PIX = 1024
TARGETS = 512
N_TGT = 64


def draw_block_owner(key, part):
    middle = jax.random.permutation(jax.random.fold_in(key, 17), N_TGT - 2)[:BLOCKS - 2] + 1
    ends = jnp.array([0, N_TGT - 1], dtype=jnp.int32)
    values = jnp.concatenate([ends, middle.astype(jnp.int32)])
    order = jax.random.permutation(jax.random.fold_in(key, 23), BLOCKS)
    return values[order].astype(jnp.int32)


def set_ends(values, key, least, high):
    place = [jax.random.randint(jax.random.fold_in(key, axis), (), 0, length) for axis, length in enumerate(values.shape)]
    longest = values.shape.index(max(values.shape))
    neighbour = place[:longest] + [(place[longest] + 1) % values.shape[longest]] + place[longest + 1:]
    return values.at[tuple(place)].set(least).at[tuple(neighbour)].set(high)


def block_levels(own_key, shape, split, smallest, high):
    def one(dim, parts):
        heights = jax.random.uniform(jax.random.fold_in(jax.random.fold_in(own_key, 6), dim), (parts,), jnp.float32, smallest / len(split), high / len(split))
        return jnp.repeat(jnp.exp(heights), shape[dim] // parts).reshape((-1,) + (1,) * (len(shape) - dim - 1))

    gain = one(*split[0])
    for cut in split[1:]:
        gain = gain * one(*cut)
    return gain


def noise(rng, shape, spread, reach, shards=(), kind=jnp.bfloat16):
    loudness = block_levels(rng, shape, shards, -0.22, 0.18) if shards else 1.0
    entries = jax.random.normal(rng, shape, jnp.float32) * spread * loudness
    return jnp.minimum(jnp.maximum(entries, -reach), reach).astype(kind)


def setup_inputs(seed: int = 0) -> dict:
    streams_of = jax.random.split(jax.random.key(seed), 6)
    return {
        "targets": noise(streams_of[0], (TARGETS, CH, PIX), 1.0, 4.0, ((0, 64),), jnp.float32),
        "labels": set_ends(jax.random.randint(streams_of[1], (TARGETS,), 0, CLASSES), jax.random.fold_in(streams_of[1], 1), 0, CLASSES - 1).astype(jnp.int32),
        "support_slots": noise(streams_of[2], (N_TGT, SB, CH, PIX), 1.0, 4.0, ((0, 64), (1, 8)), jnp.float32),
        "block_owner": draw_block_owner(jax.random.fold_in(streams_of[5], 71), 0),
        "dual_coeffs": noise(streams_of[4], (BLOCKS, SB, CLASSES), 0.03, 0.15, ((1, 8),), jnp.float32),
    }


weight_variance = 1.6
bias_variance = 0.1
loss_weight = 64.0
arcsin_scale = 2.0 / 3.141592653589793

def box_sum(states, grid_side):
    length = states.shape[-1]
    column = lax.broadcasted_iota(jnp.int32, (length,), 0) % grid_side
    zero_column = jnp.zeros(states.shape[:-1] + (1,), states.dtype)
    from_left = jnp.where(column > 0, jnp.concatenate([zero_column, states[..., :-1]], axis=-1), 0.0)
    from_right = jnp.where(column < grid_side - 1, jnp.concatenate([states[..., 1:], zero_column], axis=-1), 0.0)
    row_sum = states + from_left + from_right
    zero_row = jnp.zeros(states.shape[:-1] + (grid_side,), states.dtype)
    from_above = jnp.concatenate([zero_row, row_sum[..., :-grid_side]], axis=-1)
    from_below = jnp.concatenate([row_sum[..., grid_side:], zero_row], axis=-1)
    return row_sum + from_above + from_below

def self_chain(images):
    squares = images[:, 0, :] * images[:, 0, :]
    for channel in range(1, images.shape[1]):
        squares = squares + images[:, channel, :] * images[:, channel, :]
    variance = weight_variance * box_sum(squares / images.shape[1], SIDE) / 9.0 + bias_variance
    variances = [variance]
    for layer_index in range(1, LAYERS):
        activated = arcsin_scale * jnp.arcsin(2.0 * variance / (1.0 + 2.0 * variance))
        variance = weight_variance * box_sum(activated, SIDE) / 9.0 + bias_variance
        variances.append(variance)
    return variances

def pair_kernel(support, support_variances, targets, target_variances):
    cross_terms = targets[:, 0, :][:, None, :] * support[:, 0, :][None, :, :]
    for channel in range(1, support.shape[1]):
        cross_terms = cross_terms + targets[:, channel, :][:, None, :] * support[:, channel, :][None, :, :]
    preact = weight_variance * box_sum(cross_terms / support.shape[1], SIDE) / 9.0 + bias_variance
    tangent = preact
    activated = preact
    slope = preact
    for layer_index in range(LAYERS):
        product = (1.0 + 2.0 * target_variances[layer_index])[:, None, :] * (1.0 + 2.0 * support_variances[layer_index])[None, :, :]
        activated = arcsin_scale * jnp.arcsin(2.0 * preact / jnp.sqrt(product))
        slope = 2.0 * arcsin_scale / jnp.sqrt(product - 4.0 * preact * preact)
        if layer_index + 1 < LAYERS:
            preact_next = weight_variance * box_sum(activated, SIDE) / 9.0 + bias_variance
            tangent = preact_next + weight_variance * box_sum(tangent * slope, SIDE) / 9.0
            preact = preact_next
    return lax.optimization_barrier(jnp.mean(weight_variance * (activated + tangent * slope) + bias_variance, axis=-1))

def reference(targets, labels, support_slots, block_owner, dual_coeffs):
    support = support_slots[block_owner].reshape(BLOCKS * SB, CH, PIX)
    coeffs = dual_coeffs.reshape(BLOCKS * SB, CLASSES)
    support_variances, self_pullback = jax.vjp(self_chain, support)
    target_groups = targets.reshape(N_TGT, TGT_DEV, CH, PIX)

    def forward_group(carry, target_group):
        target_variances = self_chain(target_group)
        return (carry, pair_kernel(support, support_variances, target_group, target_variances))
    unused, kernel_rows = lax.scan(forward_group, jnp.zeros((), jnp.float32), target_groups)
    kernel_all = kernel_rows.reshape(TARGETS, BLOCKS * SB)
    predictions = jnp.dot(kernel_all, coeffs, precision=lax.Precision.HIGHEST)
    onehot = (labels[:, None] == lax.broadcasted_iota(jnp.int32, (1, CLASSES), 1)).astype(jnp.float32)
    residual_error = loss_weight * (predictions - onehot)
    pair_weights = jnp.dot(residual_error, coeffs.T, precision=lax.Precision.HIGHEST).reshape(N_TGT, TGT_DEV, BLOCKS * SB)

    def backward_group(carry, inputs):
        target_group, weights = inputs
        target_variances = self_chain(target_group)

        def kernel_rows_of(images, variances):
            return pair_kernel(images, variances, target_group, target_variances)
        unused_kernel, pullback = jax.vjp(kernel_rows_of, support, support_variances)
        grad_images, grad_variances = pullback(weights)
        summed = [total_part + grad_part for total_part, grad_part in zip(carry[1], grad_variances)]
        return ((carry[0] + grad_images, summed), None)
    initial = (jnp.zeros_like(support), [jnp.zeros_like(variance) for variance in support_variances])
    totals, unused_rows = lax.scan(backward_group, initial, (target_groups, pair_weights))
    gradient = totals[0] + self_pullback(totals[1])[0]
    return (predictions, gradient.reshape(BLOCKS, SB, CH, PIX))
```

```python
import functools

import jax
import jax.numpy as jnp
from jax import lax
from jax.experimental import pallas as pl
from jax.experimental.pallas import tpu as pltpu
from jax.sharding import PartitionSpec as P

LANES = 128
ROWS = 8
PIX = 1024
CH = 3
ALPHA = 1.6 / 9.0
W = 1.6
BIAS = 0.1
LOSS = 64.0
Q = 2.0 / 3.141592653589793

WIDE = (1.000000016156341, 0.16666297522317508, 0.07513696096432515, 0.04275936583215643,
        0.04244150116676571, -0.015453175442799802, 0.0693722411926219)
NARROW = (1.000000019010712, 0.16666188274704566, 0.07519150147740127, 0.04200062838628592,
          0.04465464851544397)


def half_arcsin(z, o, r, coefficients):
    y = z * lax.rsqrt(0.5 + 0.5 * (o * r))
    y2 = y * y
    scaled = [Q * c * 0.25**k for k, c in enumerate(coefficients)]
    total = scaled[-1]
    for c in scaled[-2::-1]:
        total = total * y2 + c
    return y * total


def lane_masks():
    lane = lax.broadcasted_iota(jnp.int32, (8, LANES), 1)
    x = lane % 32
    return (x > 0, x < 31, lane >= 32, lane < 96, [lane // 32 == k for k in range(1, 4)])


def box(v, masks):
    left, right, above, below, _ = masks
    r = []
    for a in v:
        r.append(
            a
            + jnp.where(left, pltpu.roll(a, 1, 1), 0.0)
            + jnp.where(right, pltpu.roll(a, LANES - 1, 1), 0.0)
        )
    first = jnp.where(above, pltpu.roll(r[7], 32, 1), 0.0)
    last = jnp.where(below, pltpu.roll(r[0], LANES - 32, 1), 0.0)
    r = [first] + r + [last]
    out = []
    for k in range(0, 8, 2):
        pair = r[k + 1] + r[k + 2]
        out.append(r[k] + pair)
        out.append(pair + r[k + 3])
    return out


def interleave(nat, masks):
    groups = masks[4]
    out = []
    for r in range(8):
        m, q = r // 4, r % 4
        v = None
        for y in range(4):
            a = nat[2 * y + m]
            shift = (32 * (y - q)) % LANES
            a = a if shift == 0 else pltpu.roll(a, shift, 1)
            v = a if v is None else jnp.where(groups[y - 1], a, v)
        out.append(v)
    return out


def deinterleave(v, masks):
    groups = masks[4]
    out = []
    for m in range(8):
        y, h = m // 2, m % 2
        o = None
        for q in range(4):
            a = v[4 * h + q]
            shift = (32 * (q - y)) % LANES
            a = a if shift == 0 else pltpu.roll(a, shift, 1)
            o = a if o is None else jnp.where(groups[q - 1], a, o)
        out.append(o)
    return out


def chain(channels, masks):
    squares = [a * a + b * b + d * d for a, b, d in zip(*channels)]
    n = [(ALPHA / CH) * a + BIAS for a in box(squares, masks)]
    factors, slopes = [], []
    for h in range(3):
        b = [lax.rsqrt(1.0 + 2.0 * a) for a in n]
        factors.append(b)
        if h < 2:
            act = []
            slope = []
            for a, bb in zip(n, b):
                inv = bb * bb
                z = 2.0 * a * inv
                rr = lax.rsqrt(1.0 + 4.0 * a)
                o = (1.0 + 4.0 * a) * (inv * inv)
                r = (1.0 + 2.0 * a) * rr
                act.append(half_arcsin(z, o, r, WIDE if h == 0 else NARROW))
                slope.append(2.0 * Q * inv * rr)
            slopes.append(slope)
            n = [ALPHA * a + BIAS for a in box(act, masks)]
    return factors, slopes


def main_kernel(core_ref, own_ref, other_ref, rows_ref, coef_ref, label_ref,
                parts_ref, unit_ref, tgt_ref, sup_ref, kt_ref):
    masks = lane_masks()
    core = core_ref[0]
    step = pl.program_id(0)

    @pl.when(step == 0)
    def _():
        for half, ref in enumerate((own_ref, other_ref)):
            chans = []
            for ch in range(CH):
                nat = [ref[:, ch, m * LANES:(m + 1) * LANES] for m in range(8)]
                chans.append(interleave(nat, masks))
            factors, _ = chain(chans, masks)
            for ch in range(CH):
                for r in range(8):
                    tgt_ref[half, ch, r] = chans[ch][r]
            for h in range(3):
                for r in range(8):
                    tgt_ref[half, 3 + h, r] = 2.0 * factors[h][r]
        for g in range(2):
            chans = []
            for ch in range(CH):
                nat = []
                for m in range(8):
                    pieces = [
                        rows_ref[pl.ds(m * 48 + (2 * g + b) * 3 + ch, 4, stride=12), :]
                        for b in range(2)
                    ]
                    nat.append(jnp.concatenate(pieces, axis=0))
                chans.append(interleave(nat, masks))
            factors, slopes = chain(chans, masks)
            for ch in range(CH):
                for r in range(8):
                    sup_ref[g, ch, r] = chans[ch][r]
            for h in range(3):
                for r in range(8):
                    sup_ref[g, 3 + h, r] = factors[h][r]
            for h in range(2):
                for r in range(8):
                    sup_ref[g, 6 + h, r] = slopes[h][r]
        kt_ref[...] = jnp.zeros_like(kt_ref)

    g = step // 2
    half = step % 2
    lane = lax.broadcasted_iota(jnp.int32, (8, LANES), 1)
    R = range(8)

    def pair(t, carry):
        def tgt(k, r):
            return jnp.broadcast_to(tgt_ref[half, k, r, pl.ds(t, 1), :], (8, LANES))

        def layer(h, S, theta):
            p2 = [tgt(3 + h, r) * sup_ref[g, 3 + h, r] for r in R]
            z = [p * s for p, s in zip(p2, S)]
            o = [1.0 - a * a for a in z]
            rt = [lax.rsqrt(a) for a in o]
            act = [half_arcsin(a, b, c, WIDE if h == 0 else NARROW) for a, b, c in zip(z, o, rt)]
            u = [Q * a for a in rt]
            D = [a * b for a, b in zip(p2, u)]
            f = [a * b * (c * c) for a, b, c in zip(p2, theta, rt)]
            return z, act, u, D, f

        cross = []
        for r in R:
            cross.append(tgt(0, r) * sup_ref[g, 0, r] + tgt(1, r) * sup_ref[g, 1, r]
                         + tgt(2, r) * sup_ref[g, 2, r])
        S1 = [(ALPHA / CH) * a + BIAS for a in box(cross, masks)]
        z1, A1, u1, D1, f1 = layer(0, S1, S1)
        S2 = [ALPHA * a + BIAS for a in box(A1, masks)]
        T2 = [s + ALPHA * a for s, a in zip(S2, box([x * y for x, y in zip(S1, D1)], masks))]
        z2, A2, u2, D2, f2 = layer(1, S2, T2)
        S3 = [ALPHA * a + BIAS for a in box(A2, masks)]
        T3 = [s + ALPHA * a for s, a in zip(S3, box([x * y for x, y in zip(T2, D2)], masks))]
        z3, A3, u3, D3, f3 = layer(2, S3, T3)
        total = None
        for r in R:
            term = A3[r] + T3[r] * D3[r]
            total = term if total is None else total + term
        ksum = jnp.sum(total, axis=1, keepdims=True) * (W / PIX) + BIAS
        column = half * 8 + t
        kt_ref[g] = jnp.where(lane == column, ksum, kt_ref[g])

        gt = D3
        gs = []
        for r in R:
            unit_ref[0, t, 3, r] = u3[r] * (z3[r] + f3[r])
            gs.append(D3[r] * (2.0 + z3[r] * f3[r]))
        ga = [ALPHA * a for a in box(gs, masks)]
        gp = [ALPHA * a for a in box(gt, masks)]
        gt = []
        gs = []
        for r in R:
            e = gp[r] * f2[r]
            unit_ref[0, t, 2, r] = u2[r] * (z2[r] * ga[r] + e)
            gt.append(gp[r] * D2[r])
            gs.append(D2[r] * (ga[r] + gp[r] + z2[r] * e))
        ga = [ALPHA * a for a in box(gs, masks)]
        gp = [ALPHA * a for a in box(gt, masks)]
        gs = []
        for r in R:
            e = gp[r] * f1[r]
            unit_ref[0, t, 1, r] = u1[r] * (z1[r] * ga[r] + e)
            gs.append(D1[r] * (ga[r] + gp[r] + z1[r] * e))
        gx = box(gs, masks)
        for r in R:
            unit_ref[0, t, 0, r] = gx[r]
        return carry

    lax.fori_loop(0, 8, pair, 0)

    @pl.when(step == 3)
    def _():
        part = None
        for g2 in range(2):
            rows = jnp.concatenate(
                [coef_ref[2 * g2 + b, pl.ds(core * 4, 4), :] for b in range(2)], axis=0
            )
            rows = jnp.concatenate([rows, jnp.zeros((8, LANES - rows.shape[1]), jnp.float32)], axis=1)
            term = lax.dot_general(
                kt_ref[g2], rows, (((0,), (0,)), ((), ())),
                precision=lax.Precision.HIGHEST, preferred_element_type=jnp.float32,
            )
            part = term if part is None else part + term
        own, other = part[0:8], part[8:16]
        own = jnp.where(lane == LANES - 1, label_ref[...], own)
        for peer in range(16):
            parts_ref[peer, pl.ds(pl.multiple_of(core * 8, 8), 8), :] = own
            parts_ref[peer, pl.ds(pl.multiple_of((1 - core) * 8, 8), 8), :] = other


def weigh_kernel(core_ref, parts_ref, unit_ref, tgt_ref, sup_ref, coef_ref,
                 pred_ref, grad_ref, weight_ref, acc_ref):
    masks = lane_masks()
    core = core_ref[0]
    step = pl.program_id(0)
    lane = lax.broadcasted_iota(jnp.int32, (8, LANES), 1)
    classes = coef_ref.shape[2]

    @pl.when(step == 0)
    def _():
        def total(start):
            start = pl.multiple_of(start, 8)
            v = parts_ref[0, pl.ds(start, 8), :]
            for peer in range(1, 16):
                v = v + parts_ref[peer, pl.ds(start, 8), :]
            return v

        errs = []
        for k, start in enumerate((core * 8, (1 - core) * 8)):
            v = total(start)
            label = v[:, LANES - 1:LANES]
            onehot = jnp.where(lane.astype(jnp.float32) == label, 1.0, 0.0)
            if k == 0:
                pred_ref[...] = v
            errs.append(jnp.where(lane < classes, LOSS * (v - onehot), 0.0))
        err = jnp.concatenate(errs, axis=0)
        for g in range(2):
            rows = jnp.concatenate(
                [coef_ref[2 * g + b, pl.ds(core * 4, 4), :] for b in range(2)], axis=0
            )
            rows = jnp.concatenate([rows, jnp.zeros((8, LANES - classes), jnp.float32)], axis=1)
            wt = lax.dot_general(
                rows, err, (((1,), (1,)), ((), ())),
                precision=lax.Precision.HIGHEST, preferred_element_type=jnp.float32,
            )
            for t in range(16):
                weight_ref[g, t] = jnp.broadcast_to(wt[:, t:t + 1] * (W / PIX), (8, LANES))

    g = step // 2
    half = step % 2

    def row(r, carry):
        acc = [None] * 6
        for t in range(8):
            w = weight_ref[g, half * 8 + t]
            x = w * unit_ref[0, t, 0, r]
            terms = [
                x * jnp.broadcast_to(tgt_ref[half, ch, r, t:t + 1, :], (8, LANES))
                for ch in range(CH)
            ] + [w * unit_ref[0, t, 1 + h, r] for h in range(3)]
            acc = [b if a is None else a + b for a, b in zip(acc, terms)]
        for k in range(6):
            acc_ref[half, k, r] = acc[k]
        return carry

    lax.fori_loop(0, 8, row, 0)

    @pl.when(half == 1)
    def _():
        R = range(8)

        def variance(h):
            return [
                -(sup_ref[g, 3 + h, r] * sup_ref[g, 3 + h, r])
                * (acc_ref[0, 3 + h, r] + acc_ref[1, 3 + h, r])
                for r in R
            ]

        gn = variance(2)
        for h in (1, 0):
            back = box(gn, masks)
            own = variance(h)
            gn = [own[r] + ALPHA * back[r] * sup_ref[g, 6 + h, r] for r in R]
        back = box(gn, masks)
        for ch in range(CH):
            v = [
                (ALPHA / CH) * (acc_ref[0, ch, r] + acc_ref[1, ch, r] + 2.0 * sup_ref[g, ch, r] * back[r])
                for r in R
            ]
            nat = deinterleave(v, masks)
            for m in range(8):
                for b in range(2):
                    grad_ref[pl.ds(m * 48 + (2 * g + b) * 3 + ch, 4, stride=12), :] = nat[m][4 * b:4 * b + 4]


VMEM = pltpu.MemorySpace.VMEM
SMEM = pltpu.MemorySpace.SMEM


def whole(shape):
    return pl.BlockSpec(shape, lambda i: (0,) * len(shape))


def main_call(core, own, other, rows, coef, label):
    f32 = jnp.float32
    return pl.pallas_call(
        main_kernel,
        grid=(4,),
        in_specs=[
            pl.BlockSpec(memory_space=SMEM),
            whole((8, CH, PIX)), whole((8, CH, PIX)), whole((384, LANES)),
            whole(coef.shape), whole((8, 1)),
        ],
        out_specs=[
            whole((16, 16, LANES)),
            pl.BlockSpec((1, 8, 4, 8, 8, LANES), lambda i: (i, 0, 0, 0, 0, 0)),
            whole((2, 6, 8, 8, LANES)),
            whole((2, 8, 8, 8, LANES)),
        ],
        out_shape=[
            jax.ShapeDtypeStruct((16, 16, LANES), f32),
            jax.ShapeDtypeStruct((4, 8, 4, 8, 8, LANES), f32),
            jax.ShapeDtypeStruct((2, 6, 8, 8, LANES), f32),
            jax.ShapeDtypeStruct((2, 8, 8, 8, LANES), f32),
        ],
        scratch_shapes=[pltpu.VMEM((2, 8, LANES), f32)],
        name="pairs",
    )(core, own, other, rows, coef, label)


def weigh_call(core, parts, unit, tgt, sup, coef):
    f32 = jnp.float32
    return pl.pallas_call(
        weigh_kernel,
        grid=(4,),
        in_specs=[
            pl.BlockSpec(memory_space=SMEM),
            whole((16, 16, LANES)),
            pl.BlockSpec((1, 8, 4, 8, 8, LANES), lambda i: (i, 0, 0, 0, 0, 0)),
            whole((2, 6, 8, 8, LANES)),
            whole((2, 8, 8, 8, LANES)),
            whole(coef.shape),
        ],
        out_specs=[whole((8, LANES)), whole((384, LANES))],
        out_shape=[
            jax.ShapeDtypeStruct((8, LANES), f32),
            jax.ShapeDtypeStruct((384, LANES), f32),
        ],
        scratch_shapes=[pltpu.VMEM((2, 16, 8, LANES), f32), pltpu.VMEM((2, 6, 8, 8, LANES), f32)],
        name="weigh",
    )(core, parts, unit, tgt, sup, coef)


def local(tgt_n, sup_n, targets, labels, support_slots, block_owner, dual_coeffs):
    blocks = dual_coeffs.shape[0]
    classes = dual_coeffs.shape[2]
    index = lax.axis_index("tgt")
    core = (index % 2)[None].astype(jnp.int32)
    partner = [(t, t ^ 1) for t in range(tgt_n)]
    planes = [[t for t in range(tgt_n) if t % 2 == c] for c in range(2)]
    sets = [
        [t * sup_n + s for t in (2 * k, 2 * k + 1) for s in range(sup_n)] for k in range(tgt_n // 2)
    ]
    other = lax.ppermute(targets, "tgt", partner)
    slot = support_slots[0].reshape(2, 4, CH, 8, LANES)
    slot = slot.transpose(3, 1, 0, 2, 4).reshape(tgt_n, CH, LANES)
    got = lax.all_to_all(slot, "tgt", 0, 0, tiled=True)
    mine = jnp.concatenate(
        [lax.dynamic_slice_in_dim(got, block_owner[b], 1, 0) for b in range(blocks)], axis=0
    ).reshape(1, blocks * CH, LANES)
    half_n = tgt_n // 2
    rows = lax.all_to_all(
        jnp.broadcast_to(mine, (half_n, blocks * CH, LANES)), "tgt", 0, 0,
        axis_index_groups=planes, tiled=True,
    ).reshape(half_n * blocks * CH, LANES)
    first = lax.axis_index("sup") == 0
    label = jnp.where(first, labels.astype(jnp.float32), 0.0)[:, None]
    parts, unit, tgt, sup = main_call(core, targets, other, rows, dual_coeffs, label)
    parts = lax.all_to_all(
        parts, ("tgt", "sup"), 0, 0, axis_index_groups=sets, tiled=True
    )
    pred, grad = weigh_call(core, parts, unit, tgt, sup, dual_coeffs)
    grad = lax.all_to_all(
        grad.reshape(half_n, blocks * CH, LANES), "tgt", 0, 0, axis_index_groups=planes, tiled=True
    )
    piece = jnp.sum(grad, axis=0, keepdims=True)
    full = lax.all_to_all(
        jnp.broadcast_to(piece, (half_n, blocks * CH, LANES)), "tgt", 0, 0,
        axis_index_groups=planes, tiled=True,
    )
    theirs = lax.ppermute(full, "tgt", partner)
    even = jnp.where(core[0] == 0, full, theirs)
    odd = jnp.where(core[0] == 0, theirs, full)
    both = jnp.stack([even, odd]).reshape(2, 8, 4, blocks, CH, LANES)
    out = both.transpose(3, 0, 2, 4, 1, 5).reshape(blocks, 8, CH, PIX)
    return pred[:, :classes], out


def solution(mesh):
    return jax.shard_map(
        functools.partial(local, mesh.shape["tgt"], mesh.shape["sup"]),
        mesh=mesh,
        in_specs=(
            P("tgt", None, None),
            P("tgt"),
            P("tgt", "sup", None, None),
            P(),
            P(None, "sup", None),
        ),
        out_specs=(P("tgt", None), P(None, "sup", None, None)),
        check_vma=False,
    )
```

```python
import functools

import jax
import jax.numpy as jnp
from jax import lax
from jax.experimental import pallas as pl
from jax.experimental.pallas import tpu as pltpu
from jax.sharding import PartitionSpec as P

LANES = 128
ROWS = 8
PIX = 1024
CH = 3
ALPHA = 1.6 / 9.0
W = 1.6
BIAS = 0.1
LOSS = 64.0
Q = 2.0 / 3.141592653589793

WIDE = (0.9999998602381658, 0.16669029577848243, 0.07435772061999424,
        0.05091170352566525, 0.0038116604731453715, 0.0690369823030177)
NARROW = (1.000000019010712, 0.16666188274704566, 0.07519150147740127, 0.04200062838628592,
          0.04465464851544397)


def half_arcsin(z, o, r, coefficients):
    y = z * lax.rsqrt(1.0 + o * r)
    y2 = y * y
    scaled = [2.0**0.5 * ALPHA * Q * c * 0.5**k for k, c in enumerate(coefficients)]
    total = scaled[-1]
    for c in scaled[-2::-1]:
        total = total * y2 + c
    return y * total


def lane_masks():
    lane = lax.broadcasted_iota(jnp.int32, (8, LANES), 1)
    x = lane % 32
    return (x > 0, x < 31, lane >= 32, lane < 96, [lane // 32 == k for k in range(1, 4)])


def box(v, masks):
    left, right, above, below, _ = masks
    r = []
    for a in v:
        r.append(
            a
            + jnp.where(left, pltpu.roll(a, 1, 1), 0.0)
            + jnp.where(right, pltpu.roll(a, LANES - 1, 1), 0.0)
        )
    first = jnp.where(above, pltpu.roll(r[7], 32, 1), 0.0)
    last = jnp.where(below, pltpu.roll(r[0], LANES - 32, 1), 0.0)
    r = [first] + r + [last]
    out = []
    for k in range(0, 8, 2):
        pair = r[k + 1] + r[k + 2]
        out.append(r[k] + pair)
        out.append(pair + r[k + 3])
    return out


def interleave(nat, masks):
    groups = masks[4]
    out = []
    for r in range(8):
        m, q = r // 4, r % 4
        v = None
        for y in range(4):
            a = nat[2 * y + m]
            shift = (32 * (y - q)) % LANES
            a = a if shift == 0 else pltpu.roll(a, shift, 1)
            v = a if v is None else jnp.where(groups[y - 1], a, v)
        out.append(v)
    return out


def deinterleave(v, masks):
    groups = masks[4]
    out = []
    for m in range(8):
        y, h = m // 2, m % 2
        o = None
        for q in range(4):
            a = v[4 * h + q]
            shift = (32 * (q - y)) % LANES
            a = a if shift == 0 else pltpu.roll(a, shift, 1)
            o = a if o is None else jnp.where(groups[q - 1], a, o)
        out.append(o)
    return out


def chain(channels, masks):
    squares = [a * a + b * b + d * d for a, b, d in zip(*channels)]
    n = [(ALPHA / CH) * a + BIAS for a in box(squares, masks)]
    factors, slopes = [], []
    for h in range(3):
        b = [lax.rsqrt(1.0 + 2.0 * a) for a in n]
        factors.append(b)
        if h < 2:
            act = []
            slope = []
            for a, bb in zip(n, b):
                inv = bb * bb
                z = 2.0 * a * inv
                rr = lax.rsqrt(1.0 + 4.0 * a)
                o = (1.0 + 4.0 * a) * (inv * inv)
                r = (1.0 + 2.0 * a) * rr
                act.append(half_arcsin(z, o, r, WIDE if h == 0 else NARROW))
                slope.append(2.0 * Q * inv * rr)
            slopes.append(slope)
            n = [a + BIAS for a in box(act, masks)]
    return factors, slopes


def target_kernel(images_ref, out_ref):
    masks = lane_masks()
    chans = []
    for ch in range(CH):
        nat = [images_ref[:, ch, m * LANES:(m + 1) * LANES] for m in range(8)]
        chans.append(interleave(nat, masks))
    factors, _ = chain(chans, masks)
    for r in range(8):
        for ch in range(CH):
            out_ref[ch, r] = (ALPHA / CH) * chans[ch][r]
        for h in range(3):
            out_ref[3 + h, r] = 2.0 * factors[h][r]


def coef_rows(coef_ref, core, g):
    both = []
    for b in range(2):
        rows = coef_ref[2 * g + b]
        pick = [jnp.where(core == 0, rows[2 * k:2 * k + 1], rows[2 * k + 1:2 * k + 2]) for k in range(4)]
        both.extend(pick)
    rows = jnp.concatenate(both, axis=0)
    return jnp.concatenate([rows, jnp.zeros((8, LANES - rows.shape[1]), jnp.float32)], axis=1)


def pair_chain(tgt, sup, masks, put):
    R = range(8)

    def layer(h, S, theta):
        p2 = [tgt(3 + h, r) * sup(3 + h, r) for r in R]
        z = [p * s for p, s in zip(p2, S)]
        o = [1.0 - a * a for a in z]
        rt = [lax.rsqrt(a) for a in o]
        act = [half_arcsin(a, b, c, WIDE if h == 0 else NARROW) for a, b, c in zip(z, o, rt)]
        u = [(ALPHA * Q) * a for a in rt]
        D = [a * b for a, b in zip(p2, u)]
        f = [a * b * (c * c) for a, b, c in zip(p2, theta, rt)]
        return z, act, u, D, f

    cross = [tgt(0, r) * sup(0, r) + tgt(1, r) * sup(1, r) + tgt(2, r) * sup(2, r) for r in R]
    yield
    S1 = [a + BIAS for a in box(cross, masks)]
    yield
    z1, A1, u1, D1, f1 = layer(0, S1, S1)
    yield
    back = box([x * y for x, y in zip(S1, D1)], masks)
    S2 = [a + BIAS for a in box(A1, masks)]
    T2 = [s + a for s, a in zip(S2, back)]
    yield
    z2, A2, u2, D2, f2 = layer(1, S2, T2)
    yield
    back = box([x * y for x, y in zip(T2, D2)], masks)
    S3 = [a + BIAS for a in box(A2, masks)]
    T3 = [s + a for s, a in zip(S3, back)]
    yield
    z3, A3, u3, D3, f3 = layer(2, S3, T3)
    yield
    gp = box(D3, masks)
    gs = [D3[r] * (2.0 + z3[r] * f3[r]) for r in R]
    for r in R:
        put(3, r, u3[r] * (z3[r] + f3[r]))
    ga = box(gs, masks)
    terms = [A3[r] + T3[r] * D3[r] for r in R]
    while len(terms) > 1:
        terms = [a + b for a, b in zip(terms[::2], terms[1::2])]
    entry = jnp.sum(terms[0], axis=1, keepdims=True) * (W / PIX / ALPHA) + BIAS
    yield
    gt, gs = [], []
    for r in R:
        e = gp[r] * f2[r]
        put(2, r, u2[r] * (z2[r] * ga[r] + e))
        gt.append(gp[r] * D2[r])
        gs.append(D2[r] * (ga[r] + gp[r] + z2[r] * e))
    gp = box(gt, masks)
    ga = box(gs, masks)
    yield
    gs = []
    for r in R:
        e = gp[r] * f1[r]
        put(1, r, u1[r] * (z1[r] * ga[r] + e))
        gs.append(D1[r] * (ga[r] + gp[r] + z1[r] * e))
    gx = box(gs, masks)
    for r in R:
        put(0, r, gx[r])
    yield entry


def main_kernel(core_ref, own_ref, other_ref, rows_ref, coef_ref, label_ref,
                parts_ref, unit_ref, sup_ref, kt_ref):
    masks = lane_masks()
    core = core_ref[0]
    step = pl.program_id(0)

    @pl.when(step == 0)
    def _():
        for g in range(2):
            chans = []
            for ch in range(CH):
                nat = []
                for m in range(8):
                    pieces = [
                        rows_ref[pl.ds(m * 48 + (2 * g + b) * 3 + ch, 4, stride=12), :]
                        for b in range(2)
                    ]
                    nat.append(jnp.concatenate(pieces, axis=0))
                chans.append(interleave(nat, masks))
            factors, slopes = chain(chans, masks)
            for r in range(8):
                for ch in range(CH):
                    sup_ref[g, ch, r] = chans[ch][r]
                for h in range(3):
                    sup_ref[g, 3 + h, r] = factors[h][r]
                for h in range(2):
                    sup_ref[g, 6 + h, r] = slopes[h][r]
        kt_ref[...] = jnp.zeros_like(kt_ref)

    g = step // 2
    lane = lax.broadcasted_iota(jnp.int32, (8, LANES), 1)

    def pair(i2, carry):
        def start(i, half, ref):
            t = (step % 2) * 4 + i

            def tgt(k, r):
                return jnp.broadcast_to(ref[k, r, pl.ds(t, 1), :], (8, LANES))

            def sup(k, r):
                return sup_ref[g, k, r]

            def put(k, r, value):
                unit_ref[0, i, half, k, r] = value

            return pair_chain(tgt, sup, masks, put)

        entries = None
        chains = [start(2 * i2 + j, half, ref) for j in range(2) for half, ref in enumerate((own_ref, other_ref))]
        for entries in zip(*chains):
            pass
        kt = kt_ref[g]
        for j in range(2):
            for half in range(2):
                kt = jnp.where(lane == 8 * half + (step % 2) * 4 + 2 * i2 + j, entries[2 * j + half], kt)
        kt_ref[g] = kt
        return carry

    lax.fori_loop(0, 2, pair, 0)

    @pl.when(step == 3)
    def _():
        part = None
        for g2 in range(2):
            term = lax.dot_general(
                kt_ref[g2], coef_rows(coef_ref, core, g2), (((0,), (0,)), ((), ())),
                precision=lax.Precision.HIGHEST, preferred_element_type=jnp.float32,
            )
            part = term if part is None else part + term
        own, other = part[0:8], part[8:16]
        own = jnp.where(lane == LANES - 1, label_ref[...], own)
        for peer in range(16):
            parts_ref[peer, pl.ds(pl.multiple_of(core * 8, 8), 8), :] = own
            parts_ref[peer, pl.ds(pl.multiple_of((1 - core) * 8, 8), 8), :] = other


def weigh_kernel(core_ref, parts_ref, unit_ref, own_ref, other_ref, sup_ref, coef_ref,
                 pred_ref, grad_ref, weight_ref, acc_ref):
    masks = lane_masks()
    core = core_ref[0]
    step = pl.program_id(0)
    lane = lax.broadcasted_iota(jnp.int32, (8, LANES), 1)
    classes = coef_ref.shape[2]

    @pl.when(step == 0)
    def _():
        errs = []
        for k, start in enumerate((core * 8, (1 - core) * 8)):
            start = pl.multiple_of(start, 8)
            vs = [parts_ref[peer, pl.ds(start, 8), :] for peer in range(16)]
            while len(vs) > 1:
                vs = [a + b for a, b in zip(vs[::2], vs[1::2])]
            v = vs[0]
            label = v[:, LANES - 1:LANES]
            onehot = jnp.where(lane.astype(jnp.float32) == label, 1.0, 0.0)
            if k == 0:
                pred_ref[...] = v
            errs.append(jnp.where(lane < classes, LOSS * (v - onehot), 0.0))
        err = jnp.concatenate(errs, axis=0)
        for g in range(2):
            wt = lax.dot_general(
                coef_rows(coef_ref, core, g), err, (((1,), (1,)), ((), ())),
                precision=lax.Precision.HIGHEST, preferred_element_type=jnp.float32,
            ) * (W / PIX / ALPHA)
            for t in range(16):
                weight_ref[g, t] = jnp.broadcast_to(wt[:, t:t + 1], (8, LANES))

    g = step // 2
    part = step % 2
    for r in range(8):
        acc = [None] * 6
        for i in range(4):
            for half, ref in enumerate((own_ref, other_ref)):
                t = part * 4 + i
                w = weight_ref[g, half * 8 + t]
                x = w * unit_ref[0, i, half, 0, r]
                terms = [
                    x * jnp.broadcast_to(ref[ch, r, pl.ds(t, 1), :], (8, LANES)) for ch in range(CH)
                ] + [w * unit_ref[0, i, half, 1 + h, r] for h in range(3)]
                acc = [b if a is None else a + b for a, b in zip(acc, terms)]
        for k in range(6):
            acc_ref[part, k, r] = acc[k]

    @pl.when(part == 1)
    def _():
        R = range(8)

        def variance(h):
            return [
                -(sup_ref[g, 3 + h, r] * sup_ref[g, 3 + h, r])
                * (acc_ref[0, 3 + h, r] + acc_ref[1, 3 + h, r])
                for r in R
            ]

        gn = variance(2)
        for h in (1, 0):
            back = box(gn, masks)
            own = variance(h)
            gn = [own[r] + ALPHA * back[r] * sup_ref[g, 6 + h, r] for r in R]
        back = box(gn, masks)
        for ch in range(CH):
            v = [
                acc_ref[0, ch, r] + acc_ref[1, ch, r]
                + (2.0 * ALPHA / CH) * sup_ref[g, ch, r] * back[r]
                for r in R
            ]
            nat = deinterleave(v, masks)
            for m in range(8):
                for b in range(2):
                    grad_ref[pl.ds(m * 48 + (2 * g + b) * 3 + ch, 4, stride=12), :] = nat[m][4 * b:4 * b + 4]


VMEM = pltpu.MemorySpace.VMEM
SMEM = pltpu.MemorySpace.SMEM


def whole(shape):
    return pl.BlockSpec(shape, lambda i: (0,) * len(shape))


def target_call(images):
    return pl.pallas_call(
        target_kernel,
        out_shape=jax.ShapeDtypeStruct((6, 8, 8, LANES), jnp.float32),
        name="targets",
    )(images)


UNIT = (4, 4, 2, 4, 8, 8, LANES)


def main_call(core, own, other, rows, coef, label):
    f32 = jnp.float32
    return pl.pallas_call(
        main_kernel,
        grid=(4,),
        in_specs=[
            pl.BlockSpec(memory_space=SMEM),
            whole((6, 8, 8, LANES)), whole((6, 8, 8, LANES)), whole((384, LANES)),
            whole(coef.shape), whole((8, 1)),
        ],
        out_specs=[
            whole((16, 16, LANES)),
            pl.BlockSpec((1,) + UNIT[1:], lambda i: (i,) + (0,) * 6),
            whole((2, 8, 8, 8, LANES)),
        ],
        out_shape=[
            jax.ShapeDtypeStruct((16, 16, LANES), f32),
            jax.ShapeDtypeStruct(UNIT, f32),
            jax.ShapeDtypeStruct((2, 8, 8, 8, LANES), f32),
        ],
        scratch_shapes=[pltpu.VMEM((2, 8, LANES), f32)],
        name="pairs",
    )(core, own, other, rows, coef, label)


def weigh_call(core, parts, unit, own, other, sup, coef):
    f32 = jnp.float32
    return pl.pallas_call(
        weigh_kernel,
        grid=(4,),
        in_specs=[
            pl.BlockSpec(memory_space=SMEM),
            whole((16, 16, LANES)),
            pl.BlockSpec((1,) + UNIT[1:], lambda i: (i,) + (0,) * 6),
            whole((6, 8, 8, LANES)), whole((6, 8, 8, LANES)),
            whole((2, 8, 8, 8, LANES)),
            whole(coef.shape),
        ],
        out_specs=[whole((8, LANES)), whole((384, LANES))],
        out_shape=[
            jax.ShapeDtypeStruct((8, LANES), f32),
            jax.ShapeDtypeStruct((384, LANES), f32),
        ],
        scratch_shapes=[pltpu.VMEM((2, 16, 8, LANES), f32), pltpu.VMEM((2, 6, 8, 8, LANES), f32)],
        name="weigh",
    )(core, parts, unit, own, other, sup, coef)


def local(tgt_n, sup_n, targets, labels, support_slots, block_owner, dual_coeffs):
    blocks = dual_coeffs.shape[0]
    classes = dual_coeffs.shape[2]
    index = lax.axis_index("tgt")
    core = (index % 2)[None].astype(jnp.int32)
    partner = [(t, t ^ 1) for t in range(tgt_n)]
    planes = [[t for t in range(tgt_n) if t % 2 == c] for c in range(2)]
    sets = [
        [t * sup_n + s for t in (2 * k, 2 * k + 1) for s in range(sup_n)] for k in range(tgt_n // 2)
    ]
    slot = support_slots[0].reshape(8, CH, 8, LANES)
    slot = slot.transpose(2, 0, 1, 3).reshape(tgt_n, CH, LANES)
    got = lax.all_to_all(slot, "tgt", 0, 0, tiled=True)
    own = target_call(targets)
    other = lax.ppermute(own, "tgt", partner)
    mine = jnp.concatenate(
        [lax.dynamic_slice_in_dim(got, block_owner[b], 1, 0) for b in range(blocks)], axis=0
    ).reshape(1, blocks * CH, LANES)
    half_n = tgt_n // 2
    rows = lax.all_to_all(
        jnp.broadcast_to(mine, (half_n, blocks * CH, LANES)), "tgt", 0, 0,
        axis_index_groups=planes, tiled=True,
    ).reshape(half_n * blocks * CH, LANES)
    first = lax.axis_index("sup") == 0
    label = jnp.where(first, labels.astype(jnp.float32), 0.0)[:, None]
    parts, unit, sup = main_call(core, own, other, rows, dual_coeffs, label)
    parts = lax.all_to_all(
        parts, ("tgt", "sup"), 0, 0, axis_index_groups=sets, tiled=True
    )
    pred, grad = weigh_call(core, parts, unit, own, other, sup, dual_coeffs)
    grad = lax.all_to_all(
        grad.reshape(half_n, blocks * CH, LANES), "tgt", 0, 0, axis_index_groups=planes, tiled=True
    )
    piece = jnp.sum(grad, axis=0, keepdims=True)
    full = lax.all_to_all(
        jnp.broadcast_to(piece, (half_n, blocks * CH, LANES)), "tgt", 0, 0,
        axis_index_groups=planes, tiled=True,
    )
    theirs = lax.ppermute(full, "tgt", partner)
    even = jnp.where(core[0] == 0, full, theirs)
    odd = jnp.where(core[0] == 0, theirs, full)
    both = jnp.stack([even, odd]).reshape(2, 8, 4, blocks, CH, LANES)
    out = both.transpose(3, 2, 0, 4, 1, 5).reshape(blocks, 8, CH, PIX)
    return pred[:, :classes], out


def solution(mesh):
    return jax.shard_map(
        functools.partial(local, mesh.shape["tgt"], mesh.shape["sup"]),
        mesh=mesh,
        in_specs=(
            P("tgt", None, None),
            P("tgt"),
            P("tgt", "sup", None, None),
            P(),
            P(None, "sup", None),
        ),
        out_specs=(P("tgt", None), P(None, "sup", None, None)),
        check_vma=False,
    )
```

```python
import functools

import jax
import jax.numpy as jnp
from jax import lax
from jax.experimental import pallas as pl
from jax.experimental.pallas import tpu as pltpu
from jax.sharding import PartitionSpec as P

LANES = 128
ROWS = 8
PIX = 1024
CH = 3
ALPHA = 1.6 / 9.0
W = 1.6
BIAS = 0.1
LOSS = 64.0
Q = 2.0 / 3.141592653589793

WIDE = (0.9999998602381658, 0.16669029577848243, 0.07435772061999424,
        0.05091170352566525, 0.0038116604731453715, 0.0690369823030177)
NARROW = (1.000000019010712, 0.16666188274704566, 0.07519150147740127, 0.04200062838628592,
          0.04465464851544397)


def half_arcsin(z, o, r, coefficients):
    y = z * lax.rsqrt(1.0 + o * r)
    y2 = y * y
    scaled = [2.0**0.5 * ALPHA * Q * c * 0.5**k for k, c in enumerate(coefficients)]
    total = scaled[-1]
    for c in scaled[-2::-1]:
        total = total * y2 + c
    return y * total


def lane_masks():
    lane = lax.broadcasted_iota(jnp.int32, (8, LANES), 1)
    x = lane % 32
    return (x > 0, x < 31, lane >= 32, lane < 96, [lane // 32 == k for k in range(1, 4)])


def box(v, masks):
    left, right, above, below, _ = masks
    r = []
    for a in v:
        r.append(
            a
            + jnp.where(left, pltpu.roll(a, 1, 1), 0.0)
            + jnp.where(right, pltpu.roll(a, LANES - 1, 1), 0.0)
        )
    first = jnp.where(above, pltpu.roll(r[7], 32, 1), 0.0)
    last = jnp.where(below, pltpu.roll(r[0], LANES - 32, 1), 0.0)
    r = [first] + r + [last]
    out = []
    for k in range(0, 8, 2):
        pair = r[k + 1] + r[k + 2]
        out.append(r[k] + pair)
        out.append(pair + r[k + 3])
    return out


def interleave(nat, masks):
    groups = masks[4]
    out = []
    for r in range(8):
        m, q = r // 4, r % 4
        v = None
        for y in range(4):
            a = nat[2 * y + m]
            shift = (32 * (y - q)) % LANES
            a = a if shift == 0 else pltpu.roll(a, shift, 1)
            v = a if v is None else jnp.where(groups[y - 1], a, v)
        out.append(v)
    return out


def deinterleave(v, masks):
    groups = masks[4]
    out = []
    for m in range(8):
        y, h = m // 2, m % 2
        o = None
        for q in range(4):
            a = v[4 * h + q]
            shift = (32 * (q - y)) % LANES
            a = a if shift == 0 else pltpu.roll(a, shift, 1)
            o = a if o is None else jnp.where(groups[q - 1], a, o)
        out.append(o)
    return out


def chain(channels, masks):
    squares = [a * a + b * b + d * d for a, b, d in zip(*channels)]
    n = [(ALPHA / CH) * a + BIAS for a in box(squares, masks)]
    factors, slopes = [], []
    for h in range(3):
        b = [lax.rsqrt(1.0 + 2.0 * a) for a in n]
        factors.append(b)
        if h < 2:
            act = []
            slope = []
            for a, bb in zip(n, b):
                inv = bb * bb
                z = 2.0 * a * inv
                rr = lax.rsqrt(1.0 + 4.0 * a)
                o = (1.0 + 4.0 * a) * (inv * inv)
                r = (1.0 + 2.0 * a) * rr
                act.append(half_arcsin(z, o, r, WIDE if h == 0 else NARROW))
                slope.append(2.0 * Q * inv * rr)
            slopes.append(slope)
            n = [a + BIAS for a in box(act, masks)]
    return factors, slopes


def slot_kernel(slot_ref, out_ref):
    for ch in range(CH):
        for m in range(8):
            out_ref[pl.ds(m * 32 + ch, 8, stride=4), :] = slot_ref[ch, :, m * LANES:(m + 1) * LANES]
    for m in range(8):
        out_ref[pl.ds(m * 32 + CH, 8, stride=4), :] = jnp.zeros((8, LANES), jnp.float32)


def target_kernel(core_ref, owner_ref, images_ref, coef_ref, out_ref, rows_ref, lanes_ref):
    masks = lane_masks()
    chans = []
    for ch in range(CH):
        nat = [images_ref[:, ch, m * LANES:(m + 1) * LANES] for m in range(8)]
        chans.append(interleave(nat, masks))
    factors, _ = chain(chans, masks)
    for r in range(8):
        for ch in range(CH):
            out_ref[ch, r] = (ALPHA / CH) * chans[ch][r]
        for h in range(3):
            out_ref[3 + h, r] = 2.0 * factors[h][r]
    for g in range(2):
        rows_ref[g] = coef_rows(coef_ref, core_ref[0], g)
    for b in range(owner_ref.shape[0]):
        lanes_ref[b:b + 1, :] = jnp.full((1, LANES), owner_ref[b], jnp.int32)


def coef_rows(coef_ref, core, g):
    both = []
    for b in range(2):
        rows = coef_ref[2 * g + b]
        pick = [jnp.where(core == 0, rows[2 * k:2 * k + 1], rows[2 * k + 1:2 * k + 2]) for k in range(4)]
        both.extend(pick)
    rows = jnp.concatenate(both, axis=0)
    return jnp.concatenate([rows, jnp.zeros((8, LANES - rows.shape[1]), jnp.float32)], axis=1)


def pair_chain(tgt, sup, masks, put):
    R = range(8)

    def layer(h, S, theta):
        p2 = [tgt(3 + h, r) * sup(3 + h, r) for r in R]
        z = [p * s for p, s in zip(p2, S)]
        o = [1.0 - a * a for a in z]
        rt = [lax.rsqrt(a) for a in o]
        act = [half_arcsin(a, b, c, WIDE if h == 0 else NARROW) for a, b, c in zip(z, o, rt)]
        u = [(ALPHA * Q) * a for a in rt]
        D = [a * b for a, b in zip(p2, u)]
        f = [a * b * (c * c) for a, b, c in zip(p2, theta, rt)]
        return z, act, u, D, f

    cross = [tgt(0, r) * sup(0, r) + tgt(1, r) * sup(1, r) + tgt(2, r) * sup(2, r) for r in R]
    yield
    S1 = [a + BIAS for a in box(cross, masks)]
    yield
    z1, A1, u1, D1, f1 = layer(0, S1, S1)
    yield
    back = box([x * y for x, y in zip(S1, D1)], masks)
    S2 = [a + BIAS for a in box(A1, masks)]
    T2 = [s + a for s, a in zip(S2, back)]
    yield
    z2, A2, u2, D2, f2 = layer(1, S2, T2)
    yield
    back = box([x * y for x, y in zip(T2, D2)], masks)
    S3 = [a + BIAS for a in box(A2, masks)]
    T3 = [s + a for s, a in zip(S3, back)]
    yield
    z3, A3, u3, D3, f3 = layer(2, S3, T3)
    yield
    gp = box(D3, masks)
    gs = [D3[r] * (2.0 + z3[r] * f3[r]) for r in R]
    for r in R:
        put(3, r, u3[r] * (z3[r] + f3[r]))
    ga = box(gs, masks)
    terms = [A3[r] + T3[r] * D3[r] for r in R]
    while len(terms) > 1:
        terms = [a + b for a, b in zip(terms[::2], terms[1::2])]
    entry = jnp.sum(terms[0], axis=1, keepdims=True) * (W / PIX / ALPHA) + BIAS
    yield
    gt, gs = [], []
    for r in R:
        e = gp[r] * f2[r]
        put(2, r, u2[r] * (z2[r] * ga[r] + e))
        gt.append(gp[r] * D2[r])
        gs.append(D2[r] * (ga[r] + gp[r] + z2[r] * e))
    gp = box(gt, masks)
    ga = box(gs, masks)
    yield
    gs = []
    for r in R:
        e = gp[r] * f1[r]
        put(1, r, u1[r] * (z1[r] * ga[r] + e))
        gs.append(D1[r] * (ga[r] + gp[r] + z1[r] * e))
    gx = box(gs, masks)
    for r in R:
        put(0, r, gx[r])
    yield entry


def main_kernel(core_ref, own_ref, other_ref, rows_ref, coef_ref, label_ref,
                parts_ref, unit_ref, sup_ref, kt_ref):
    masks = lane_masks()
    core = core_ref[0]
    step = pl.program_id(0)

    @pl.when(step == 0)
    def _():
        for g in range(2):
            chans = []
            for ch in range(CH):
                nat = []
                for m in range(8):
                    pieces = [
                        rows_ref[pl.ds(m * 48 + ch * 4 + 2 * g + b, 4, stride=12), :]
                        for b in range(2)
                    ]
                    nat.append(jnp.concatenate(pieces, axis=0))
                chans.append(interleave(nat, masks))
            factors, slopes = chain(chans, masks)
            for r in range(8):
                for ch in range(CH):
                    sup_ref[g, ch, r] = chans[ch][r]
                for h in range(3):
                    sup_ref[g, 3 + h, r] = factors[h][r]
                for h in range(2):
                    sup_ref[g, 6 + h, r] = slopes[h][r]
        kt_ref[...] = jnp.zeros_like(kt_ref)

    g = step // 2
    lane = lax.broadcasted_iota(jnp.int32, (8, LANES), 1)

    def pair(i2, carry):
        def start(i, half, ref):
            t = (step % 2) * 4 + i

            def tgt(k, r):
                return jnp.broadcast_to(ref[k, r, pl.ds(t, 1), :], (8, LANES))

            def sup(k, r):
                return sup_ref[g, k, r]

            def put(k, r, value):
                unit_ref[step, i, half, k, r] = value

            return pair_chain(tgt, sup, masks, put)

        entries = None
        chains = [start(2 * i2 + j, half, ref) for j in range(2) for half, ref in enumerate((own_ref, other_ref))]
        for entries in zip(*chains):
            pass
        kt = kt_ref[g]
        for j in range(2):
            for half in range(2):
                kt = jnp.where(lane == 8 * half + (step % 2) * 4 + 2 * i2 + j, entries[2 * j + half], kt)
        kt_ref[g] = kt
        return carry

    lax.fori_loop(0, 2, pair, 0)

    @pl.when(step == 3)
    def _():
        part = None
        for g2 in range(2):
            term = lax.dot_general(
                kt_ref[g2], coef_ref[g2], (((0,), (0,)), ((), ())),
                precision=lax.Precision.HIGHEST, preferred_element_type=jnp.float32,
            )
            part = term if part is None else part + term
        own, other = part[0:8], part[8:16]
        own = jnp.where(lane == LANES - 1, label_ref[...], own)
        for peer in range(16):
            parts_ref[peer, pl.ds(pl.multiple_of(core * 8, 8), 8), :] = own
            parts_ref[peer, pl.ds(pl.multiple_of((1 - core) * 8, 8), 8), :] = other


def weigh_kernel(classes, core_ref, parts_ref, unit_ref, own_ref, other_ref, sup_ref, coef_ref,
                 pred_ref, grad_ref, weight_ref, acc_ref):
    masks = lane_masks()
    core = core_ref[0]
    step = pl.program_id(0)
    lane = lax.broadcasted_iota(jnp.int32, (8, LANES), 1)

    @pl.when(step == 0)
    def _():
        errs = []
        for k, start in enumerate((core * 8, (1 - core) * 8)):
            start = pl.multiple_of(start, 8)
            vs = [parts_ref[peer, pl.ds(start, 8), :] for peer in range(16)]
            while len(vs) > 1:
                vs = [a + b for a, b in zip(vs[::2], vs[1::2])]
            v = vs[0]
            label = v[:, LANES - 1:LANES]
            onehot = jnp.where(lane.astype(jnp.float32) == label, 1.0, 0.0)
            if k == 0:
                pred_ref[...] = v
            errs.append(jnp.where(lane < classes, LOSS * (v - onehot), 0.0))
        err = jnp.concatenate(errs, axis=0)
        for g in range(2):
            wt = lax.dot_general(
                coef_ref[g], err, (((1,), (1,)), ((), ())),
                precision=lax.Precision.HIGHEST, preferred_element_type=jnp.float32,
            ) * (W / PIX / ALPHA)
            for t in range(16):
                weight_ref[g, t] = jnp.broadcast_to(wt[:, t:t + 1], (8, LANES))

    g = step // 2
    part = step % 2
    for r in range(8):
        acc = [None] * 6
        for i in range(4):
            for half, ref in enumerate((own_ref, other_ref)):
                t = part * 4 + i
                w = weight_ref[g, half * 8 + t]
                x = w * unit_ref[step, i, half, 0, r]
                terms = [
                    x * jnp.broadcast_to(ref[ch, r, pl.ds(t, 1), :], (8, LANES)) for ch in range(CH)
                ] + [w * unit_ref[step, i, half, 1 + h, r] for h in range(3)]
                acc = [b if a is None else a + b for a, b in zip(acc, terms)]
        for k in range(6):
            acc_ref[part, k, r] = acc[k]

    @pl.when(part == 1)
    def _():
        R = range(8)

        def variance(h):
            return [
                -(sup_ref[g, 3 + h, r] * sup_ref[g, 3 + h, r])
                * (acc_ref[0, 3 + h, r] + acc_ref[1, 3 + h, r])
                for r in R
            ]

        gn = variance(2)
        for h in (1, 0):
            back = box(gn, masks)
            own = variance(h)
            gn = [own[r] + ALPHA * back[r] * sup_ref[g, 6 + h, r] for r in R]
        back = box(gn, masks)
        for ch in range(CH):
            v = [
                acc_ref[0, ch, r] + acc_ref[1, ch, r]
                + (2.0 * ALPHA / CH) * sup_ref[g, ch, r] * back[r]
                for r in R
            ]
            nat = deinterleave(v, masks)
            for m in range(8):
                for b in range(2):
                    grad_ref[pl.ds(m * 48 + ch * 4 + 2 * g + b, 4, stride=12), :] = nat[m][4 * b:4 * b + 4]


VMEM = pltpu.MemorySpace.VMEM
SMEM = pltpu.MemorySpace.SMEM
FULL = pl.BlockSpec(memory_space=VMEM)
PARAMS = pltpu.CompilerParams(vmem_limit_bytes=24 * 2**20)


def slot_call(slot):
    return pl.pallas_call(
        slot_kernel,
        in_specs=[FULL], out_specs=FULL,
        out_shape=jax.ShapeDtypeStruct((256, LANES), jnp.float32),
        compiler_params=PARAMS,
        name="slot",
    )(slot)


def target_call(core, owner, images, coef):
    f32 = jnp.float32
    return pl.pallas_call(
        target_kernel,
        in_specs=[pl.BlockSpec(memory_space=SMEM)] * 2 + [FULL, FULL],
        out_specs=[FULL] * 3,
        out_shape=[
            jax.ShapeDtypeStruct((6, 8, 8, LANES), f32),
            jax.ShapeDtypeStruct((2, 8, LANES), f32),
            jax.ShapeDtypeStruct((owner.shape[0], LANES), jnp.int32),
        ],
        compiler_params=PARAMS,
        name="targets",
    )(core, owner, images, coef)


def pick_kernel(owner_ref, got_ref, out_ref):
    blocks = [jnp.zeros(got_ref.shape[1:], jnp.float32)] * owner_ref.shape[0]
    owners = [jnp.broadcast_to(owner_ref[b:b + 1, :], got_ref.shape[1:]) for b in range(len(blocks))]
    for slot in range(got_ref.shape[0]):
        v = got_ref[slot]
        blocks = [jnp.where(o == slot, v, a) for o, a in zip(owners, blocks)]
    piece = [v[ch:ch + 1] for ch in range(CH) for v in blocks]
    twice = jnp.concatenate(piece + piece, axis=0)
    for k in range(out_ref.shape[0] // twice.shape[0]):
        out_ref[k * twice.shape[0]:(k + 1) * twice.shape[0], :] = twice


def pick_call(owner, got, count):
    return pl.pallas_call(
        pick_kernel,
        in_specs=[FULL, FULL],
        out_specs=FULL,
        out_shape=jax.ShapeDtypeStruct((count * CH * owner.shape[0], LANES), jnp.float32),
        compiler_params=PARAMS,
        name="pick",
    )(owner, got)


UNIT = (4, 4, 2, 4, 8, 8, LANES)


def main_call(core, own, other, rows, coef, label):
    f32 = jnp.float32
    return pl.pallas_call(
        main_kernel,
        grid=(4,),
        in_specs=[
            pl.BlockSpec(memory_space=SMEM),
            FULL, FULL, FULL,
            FULL, FULL,
        ],
        out_specs=[
            FULL,
            FULL,
            FULL,
        ],
        out_shape=[
            jax.ShapeDtypeStruct((16, 16, LANES), f32),
            jax.ShapeDtypeStruct(UNIT, f32),
            jax.ShapeDtypeStruct((2, 8, 8, 8, LANES), f32),
        ],
        scratch_shapes=[pltpu.VMEM((2, 8, LANES), f32)],
        compiler_params=PARAMS,
        name="pairs",
    )(core, own, other, rows, coef, label)


def weigh_call(classes, core, parts, unit, own, other, sup, coef):
    f32 = jnp.float32
    return pl.pallas_call(
        functools.partial(weigh_kernel, classes),
        grid=(4,),
        in_specs=[
            pl.BlockSpec(memory_space=SMEM),
            FULL,
            FULL,
            FULL, FULL,
            FULL,
            FULL,
        ],
        out_specs=[FULL, FULL],
        out_shape=[
            jax.ShapeDtypeStruct((8, LANES), f32),
            jax.ShapeDtypeStruct((384, LANES), f32),
        ],
        scratch_shapes=[pltpu.VMEM((2, 16, 8, LANES), f32), pltpu.VMEM((2, 6, 8, 8, LANES), f32)],
        compiler_params=PARAMS,
        name="weigh",
    )(core, parts, unit, own, other, sup, coef)


def local(tgt_n, sup_n, targets, labels, support_slots, block_owner, dual_coeffs):
    blocks = dual_coeffs.shape[0]
    classes = dual_coeffs.shape[2]
    index = lax.axis_index("tgt")
    core = (index % 2)[None].astype(jnp.int32)
    partner = [(t, t ^ 1) for t in range(tgt_n)]
    planes = [[t for t in range(tgt_n) if t % 2 == c] for c in range(2)]
    sets = [
        [t * sup_n + s for t in (2 * k, 2 * k + 1) for s in range(sup_n)] for k in range(tgt_n // 2)
    ]
    slot = slot_call(support_slots[0].transpose(1, 0, 2)).reshape(tgt_n, 4, LANES)
    got = lax.all_to_all(slot, "tgt", 0, 0, tiled=True)
    own, coef, owner = target_call(core, block_owner, targets, dual_coeffs)
    got, own, owner = lax.optimization_barrier((got, own, owner))
    other = lax.ppermute(own, "tgt", partner)
    half_n = tgt_n // 2
    piece_shape = (half_n, CH, blocks, LANES)
    rows = lax.all_to_all(
        pick_call(owner, got, half_n).reshape(piece_shape), "tgt", 0, 0,
        axis_index_groups=planes, tiled=True,
    ).reshape(half_n * blocks * CH, LANES)
    first = lax.axis_index("sup") == 0
    label = jnp.where(first, labels.astype(jnp.float32), 0.0)[:, None]
    parts, unit, sup = main_call(core, own, other, rows, coef, label)
    parts = lax.all_to_all(
        parts, ("tgt", "sup"), 0, 0, axis_index_groups=sets, tiled=True
    )
    pred, grad = weigh_call(classes, core, parts, unit, own, other, sup, coef)
    grad = lax.all_to_all(
        grad.reshape(piece_shape), "tgt", 0, 0, axis_index_groups=planes, tiled=True
    )
    piece = jnp.sum(grad, axis=0, keepdims=True)
    full = lax.all_to_all(
        jnp.broadcast_to(piece, piece_shape), "tgt", 0, 0, axis_index_groups=planes, tiled=True
    )
    theirs = lax.ppermute(full, "tgt", partner)
    even = jnp.where(core[0] == 0, full, theirs)
    odd = jnp.where(core[0] == 0, theirs, full)
    both = jnp.stack([even, odd]).reshape(2, 8, 4, CH, blocks, LANES)
    out = both.transpose(4, 2, 0, 3, 1, 5).reshape(blocks, 8, CH, PIX)
    return pred[:, :classes], out


def solution(mesh):
    return jax.shard_map(
        functools.partial(local, mesh.shape["tgt"], mesh.shape["sup"]),
        mesh=mesh,
        in_specs=(
            P("tgt", None, None),
            P("tgt"),
            P("tgt", "sup", None, None),
            P(),
            P(None, "sup", None),
        ),
        out_specs=(P("tgt", None), P(None, "sup", None, None)),
        check_vma=False,
    )
```

```python
import functools

import jax
import jax.numpy as jnp
from jax import lax
from jax.experimental import pallas as pl
from jax.experimental.pallas import tpu as pltpu
from jax.sharding import PartitionSpec as P

LANES = 128
PIX = 1024
CH = 3
ALPHA = 1.6 / 9.0
W = 1.6
BIAS = 0.1
LOSS = 64.0
Q = 2.0 / 3.141592653589793

WIDE = (0.9999998602381658, 0.16669029577848243, 0.07435772061999424,
        0.05091170352566525, 0.0038116604731453715, 0.0690369823030177)
NARROW = (1.000000019010712, 0.16666188274704566, 0.07519150147740127, 0.04200062838628592,
          0.04465464851544397)


def half_arcsin(z, o, r, coefficients):
    y = z * lax.rsqrt(1.0 + o * r)
    y2 = y * y
    scaled = [2.0**0.5 * c * 0.5**k for k, c in enumerate(coefficients)]
    total = scaled[-1]
    for c in scaled[-2::-1]:
        total = total * y2 + c
    return y * total


def lane_masks():
    lane = lax.broadcasted_iota(jnp.int32, (8, LANES), 1)
    edges = (lane % 8 > 0, lane % 8 < 7, lane >= 8, lane < LANES - 8)
    k, h, c = lane // 16, lane // 8 % 2, lane % 8
    tiled = (2 * h + k // 4) * 32 + 4 * c + k % 4
    row, col = lane // 32, lane % 32
    natural = ((row % 2) * 4 + col % 4) * 16 + (row // 2) * 8 + col // 4
    swap = [(lane // (16 * bit)) % 2 == 1 for bit in (1, 2, 4)]
    return edges, tiled, natural, swap


def box(v, masks):
    left, right, above, below = masks[0]
    r = []
    for i in (0, 4):
        c0, c1, c2, c3 = v[i:i + 4]
        p, q = c0 + c1, c2 + c3
        r.append(p + jnp.where(left, pltpu.roll(c3, 1, 1), 0.0))
        r.append(p + c2)
        r.append(c1 + q)
        r.append(q + jnp.where(right, pltpu.roll(c0, LANES - 1, 1), 0.0))
    out = [None] * 8
    for j in range(4):
        a, b = r[j], r[4 + j]
        p = a + b
        out[j] = p + jnp.where(above, pltpu.roll(b, 8, 1), 0.0)
        out[4 + j] = p + jnp.where(below, pltpu.roll(a, LANES - 8, 1), 0.0)
    return out


def exchange_blocks(v, masks):
    v = list(v)
    for n, bit in enumerate((1, 2, 4)):
        odd = masks[3][n]
        for i in range(8):
            if not i & bit:
                a, b = v[i], v[i + bit]
                v[i] = jnp.where(odd, pltpu.roll(b, 16 * bit, 1), a)
                v[i + bit] = jnp.where(odd, b, pltpu.roll(a, LANES - 16 * bit, 1))
    return v


def interleave(nat, masks):
    return exchange_blocks([jnp.take_along_axis(a, masks[1], axis=1) for a in nat], masks)


def chain(channels, masks):
    squares = [a * a + b * b + d * d for a, b, d in zip(*channels)]
    n = [(ALPHA / CH) * a + BIAS for a in box(squares, masks)]
    factors, slopes = [], []
    for h in range(3):
        b = [lax.rsqrt(1.0 + 2.0 * a) for a in n]
        factors.append(b)
        if h < 2:
            act = []
            slope = []
            for a, bb in zip(n, b):
                inv = bb * bb
                z = 2.0 * a * inv
                rr = lax.rsqrt(1.0 + 4.0 * a)
                o = (1.0 + 4.0 * a) * (inv * inv)
                r = (1.0 + 2.0 * a) * rr
                act.append(half_arcsin(z, o, r, WIDE if h == 0 else NARROW))
                slope.append(2.0 * Q * inv * rr)
            slopes.append(slope)
            n = [(ALPHA * Q) * a + BIAS for a in box(act, masks)]
    return factors, slopes


def slot_kernel(slot_ref, out_ref):
    for ch in range(CH):
        for m in range(8):
            out_ref[pl.ds(m * 32 + ch, 8, stride=4), :] = slot_ref[ch, :, m * LANES:(m + 1) * LANES]
    for m in range(8):
        out_ref[pl.ds(m * 32 + CH, 8, stride=4), :] = jnp.zeros((8, LANES), jnp.float32)


def target_kernel(core_ref, owner_ref, images_ref, coef_ref, out_ref, rows_ref, lanes_ref):
    masks = lane_masks()
    chans = []
    for ch in range(CH):
        nat = [images_ref[:, ch, m * LANES:(m + 1) * LANES] for m in range(8)]
        chans.append(interleave(nat, masks))
    factors, _ = chain(chans, masks)
    for r in range(8):
        for ch in range(CH):
            out_ref[ch, r] = (1.0 / (CH * Q)) * chans[ch][r]
        for h in range(3):
            out_ref[3 + h, r] = (2.0 * ALPHA * Q) * factors[h][r]
    for g in range(2):
        rows_ref[g] = coef_rows(coef_ref, core_ref[0], g)
    for b in range(owner_ref.shape[0]):
        lanes_ref[b:b + 1, :] = jnp.full((1, LANES), owner_ref[b], jnp.int32)


def coef_rows(coef_ref, core, g):
    both = []
    for b in range(2):
        rows = coef_ref[2 * g + b]
        pick = [jnp.where(core == 0, rows[2 * k:2 * k + 1], rows[2 * k + 1:2 * k + 2]) for k in range(4)]
        both.extend(pick)
    rows = jnp.concatenate(both, axis=0)
    return jnp.concatenate([rows, jnp.zeros((8, LANES - rows.shape[1]), jnp.float32)], axis=1)


def pair_chain(tgt, sup, masks, put):
    R = range(8)

    def layer(h, S, theta):
        p2 = [tgt(3 + h, r) * sup(3 + h, r) for r in R]
        z = [p * s for p, s in zip(p2, S)]
        o = [1.0 - a * a for a in z]
        rt = [lax.rsqrt(a) for a in o]
        act = [half_arcsin(a, b, c, WIDE if h == 0 else NARROW) for a, b, c in zip(z, o, rt)]
        D = [a * b for a, b in zip(p2, rt)]
        f = [a * b * (c * c) for a, b, c in zip(p2, theta, rt)]
        return z, act, rt, D, f

    cross = [tgt(0, r) * sup(0, r) + tgt(1, r) * sup(1, r) + tgt(2, r) * sup(2, r) for r in R]
    yield
    S1 = [a + BIAS / (ALPHA * Q) for a in box(cross, masks)]
    yield
    z1, A1, u1, D1, f1 = layer(0, S1, S1)
    yield
    back = box([x * y for x, y in zip(S1, D1)], masks)
    S2 = [a + BIAS / (ALPHA * Q) for a in box(A1, masks)]
    T2 = [s + a for s, a in zip(S2, back)]
    yield
    z2, A2, u2, D2, f2 = layer(1, S2, T2)
    yield
    back = box([x * y for x, y in zip(T2, D2)], masks)
    S3 = [a + BIAS / (ALPHA * Q) for a in box(A2, masks)]
    T3 = [s + a for s, a in zip(S3, back)]
    yield
    z3, A3, u3, D3, f3 = layer(2, S3, T3)
    yield
    gp = box(D3, masks)
    gs = [D3[r] * (2.0 + z3[r] * f3[r]) for r in R]
    for r in R:
        put(3, r, u3[r] * (z3[r] + f3[r]))
    ga = box(gs, masks)
    terms = [A3[r] + T3[r] * D3[r] for r in R]
    while len(terms) > 1:
        terms = [a + b for a, b in zip(terms[::2], terms[1::2])]
    entry = jnp.sum(terms[0], axis=1, keepdims=True) * (W * Q / PIX) + BIAS
    yield
    gt, gs = [], []
    for r in R:
        e = gp[r] * f2[r]
        put(2, r, u2[r] * (z2[r] * ga[r] + e))
        gt.append(gp[r] * D2[r])
        gs.append(D2[r] * (ga[r] + gp[r] + z2[r] * e))
    gp = box(gt, masks)
    ga = box(gs, masks)
    yield
    gs = []
    for r in R:
        e = gp[r] * f1[r]
        put(1, r, u1[r] * (z1[r] * ga[r] + e))
        gs.append(D1[r] * (ga[r] + gp[r] + z1[r] * e))
    gx = box(gs, masks)
    for r in R:
        put(0, r, gx[r])
    yield entry


def main_kernel(core_ref, own_ref, other_ref, rows_ref, coef_ref, label_ref,
                parts_ref, unit_ref, sup_ref, kt_ref):
    masks = lane_masks()
    core = core_ref[0]
    step = pl.program_id(0)

    @pl.when(step == 0)
    def _():
        for g in range(2):
            chans = []
            for ch in range(CH):
                nat = []
                for m in range(8):
                    pieces = [
                        rows_ref[pl.ds(m * 48 + ch * 4 + 2 * g + b, 4, stride=12), :]
                        for b in range(2)
                    ]
                    nat.append(jnp.concatenate(pieces, axis=0))
                chans.append(exchange_blocks(nat, masks))
            factors, slopes = chain(chans, masks)
            for r in range(8):
                for ch in range(CH):
                    sup_ref[g, ch, r] = chans[ch][r]
                for h in range(3):
                    sup_ref[g, 3 + h, r] = factors[h][r]
                for h in range(2):
                    sup_ref[g, 6 + h, r] = slopes[h][r]
        kt_ref[...] = jnp.zeros_like(kt_ref)

    g = step // 2
    lane = lax.broadcasted_iota(jnp.int32, (8, LANES), 1)

    def pair(i2, carry):
        def start(i, half, ref):
            t = (step % 2) * 4 + i

            def tgt(k, r):
                return jnp.broadcast_to(ref[k, r, pl.ds(t, 1), :], (8, LANES))

            def sup(k, r):
                return sup_ref[g, k, r]

            def put(k, r, value):
                unit_ref[step, i, half, k, r] = value

            return pair_chain(tgt, sup, masks, put)

        entries = None
        chains = [start(2 * i2 + j, half, ref) for j in range(2) for half, ref in enumerate((own_ref, other_ref))]
        for entries in zip(*chains):
            pass
        kt = kt_ref[g]
        for j in range(2):
            for half in range(2):
                kt = jnp.where(lane == 8 * half + (step % 2) * 4 + 2 * i2 + j, entries[2 * j + half], kt)
        kt_ref[g] = kt
        return carry

    lax.fori_loop(0, 2, pair, 0)

    @pl.when(step == 3)
    def _():
        part = None
        for g2 in range(2):
            term = lax.dot_general(
                kt_ref[g2], coef_ref[g2], (((0,), (0,)), ((), ())),
                precision=lax.Precision.HIGHEST, preferred_element_type=jnp.float32,
            )
            part = term if part is None else part + term
        own, other = part[0:8], part[8:16]
        own = jnp.where(lane == LANES - 1, label_ref[...], own)
        for peer in range(16):
            parts_ref[peer, pl.ds(pl.multiple_of(core * 8, 8), 8), :] = own
            parts_ref[peer, pl.ds(pl.multiple_of((1 - core) * 8, 8), 8), :] = other


def weigh_kernel(classes, core_ref, parts_ref, unit_ref, own_ref, other_ref, sup_ref, coef_ref,
                 grad_ref, weight_ref, acc_ref):
    masks = lane_masks()
    core = core_ref[0]
    step = pl.program_id(0)
    lane = lax.broadcasted_iota(jnp.int32, (8, LANES), 1)

    @pl.when(step == 0)
    def _():
        errs = []
        for start in (core * 8, (1 - core) * 8):
            start = pl.multiple_of(start, 8)
            vs = [parts_ref[peer, pl.ds(start, 8), :] for peer in range(16)]
            while len(vs) > 1:
                vs = [a + b for a, b in zip(vs[::2], vs[1::2])]
            v = vs[0]
            label = v[:, LANES - 1:LANES]
            onehot = jnp.where(lane.astype(jnp.float32) == label, 1.0, 0.0)
            errs.append(jnp.where(lane < classes, LOSS * (v - onehot), 0.0))
        err = jnp.concatenate(errs, axis=0)
        for g in range(2):
            wt = lax.dot_general(
                coef_ref[g], err, (((1,), (1,)), ((), ())),
                precision=lax.Precision.HIGHEST, preferred_element_type=jnp.float32,
            ) * (W * Q / PIX)
            for t in range(16):
                weight_ref[g, t] = jnp.broadcast_to(wt[:, t:t + 1], (8, LANES))

    g = step // 2
    part = step % 2
    for r in range(8):
        acc = [None] * 6
        for i in range(4):
            for half, ref in enumerate((own_ref, other_ref)):
                t = part * 4 + i
                w = weight_ref[g, half * 8 + t]
                x = w * unit_ref[step, i, half, 0, r]
                terms = [
                    x * jnp.broadcast_to(ref[ch, r, pl.ds(t, 1), :], (8, LANES)) for ch in range(CH)
                ] + [w * unit_ref[step, i, half, 1 + h, r] for h in range(3)]
                acc = [b if a is None else a + b for a, b in zip(acc, terms)]
        for k in range(6):
            acc_ref[step, k, r] = acc[k]

    @pl.when(step == 3)
    def _():
        R = range(8)

        def variance(g, h):
            return [
                -(sup_ref[g, 3 + h, r] * sup_ref[g, 3 + h, r])
                * (acc_ref[2 * g, 3 + h, r] + acc_ref[2 * g + 1, 3 + h, r])
                for r in R
            ]

        G = range(2)
        gn = [variance(g, 2) for g in G]
        for h in (1, 0):
            back = [box(gn[g], masks) for g in G]
            own = [variance(g, h) for g in G]
            gn = [[own[g][r] + ALPHA * back[g][r] * sup_ref[g, 6 + h, r] for r in R] for g in G]
        back = [box(gn[g], masks) for g in G]
        for ch in range(CH):
            for g in G:
                v = [
                    acc_ref[2 * g, ch, r] + acc_ref[2 * g + 1, ch, r]
                    + (2.0 * ALPHA / CH) * sup_ref[g, ch, r] * back[g][r]
                    for r in R
                ]
                nat = exchange_blocks(v, masks)
                for m in range(8):
                    for b in range(2):
                        grad_ref[pl.ds(m * 48 + ch * 4 + 2 * g + b, 4, stride=12), :] = nat[m][4 * b:4 * b + 4]


VMEM = pltpu.MemorySpace.VMEM
SMEM = pltpu.MemorySpace.SMEM
FULL = pl.BlockSpec(memory_space=VMEM)
PARAMS = pltpu.CompilerParams(vmem_limit_bytes=24 * 2**20)


def fold_kernel(parts_ref, out_ref):
    vs = [parts_ref[k * 24:k * 24 + 24, :] for k in range(parts_ref.shape[0] // 24)]
    while len(vs) > 1:
        vs = [a + b for a, b in zip(vs[::2], vs[1::2])]
    half = vs[0].shape[0] // 2
    piece = vs[0][:half] + vs[0][half:]
    twice = jnp.concatenate([piece, piece], axis=0)
    natural = jnp.broadcast_to(lane_masks()[2][0:1], twice.shape)
    twice = jnp.take_along_axis(twice, natural, axis=1)
    for k in range(out_ref.shape[0] // 24):
        out_ref[k * 24:k * 24 + 24, :] = twice


def fold_call(parts):
    return pl.pallas_call(
        fold_kernel,
        in_specs=[FULL], out_specs=FULL,
        out_shape=jax.ShapeDtypeStruct(parts.shape, jnp.float32),
        compiler_params=PARAMS,
        name="fold",
    )(parts)


def slot_call(slot):
    return pl.pallas_call(
        slot_kernel,
        in_specs=[FULL], out_specs=FULL,
        out_shape=jax.ShapeDtypeStruct((256, LANES), jnp.float32),
        compiler_params=PARAMS,
        name="slot",
    )(slot)


def target_call(core, owner, images, coef):
    f32 = jnp.float32
    return pl.pallas_call(
        target_kernel,
        in_specs=[pl.BlockSpec(memory_space=SMEM)] * 2 + [FULL, FULL],
        out_specs=[FULL] * 3,
        out_shape=[
            jax.ShapeDtypeStruct((6, 8, 8, LANES), f32),
            jax.ShapeDtypeStruct((2, 8, LANES), f32),
            jax.ShapeDtypeStruct((owner.shape[0], LANES), jnp.int32),
        ],
        compiler_params=PARAMS,
        name="targets",
    )(core, owner, images, coef)


def pick_kernel(owner_ref, got_ref, out_ref):
    blocks = [jnp.zeros(got_ref.shape[1:], jnp.float32)] * owner_ref.shape[0]
    owners = [jnp.broadcast_to(owner_ref[b:b + 1, :], got_ref.shape[1:]) for b in range(len(blocks))]
    for slot in range(got_ref.shape[0]):
        v = got_ref[slot]
        blocks = [jnp.where(o == slot, v, a) for o, a in zip(owners, blocks)]
    piece = [v[ch:ch + 1] for ch in range(CH) for v in blocks]
    twice = jnp.concatenate(piece + piece, axis=0)
    tiled = jnp.broadcast_to(lane_masks()[1][0:1], twice.shape)
    twice = jnp.take_along_axis(twice, tiled, axis=1)
    for k in range(out_ref.shape[0] // twice.shape[0]):
        out_ref[k * twice.shape[0]:(k + 1) * twice.shape[0], :] = twice


def pick_call(owner, got, count):
    return pl.pallas_call(
        pick_kernel,
        in_specs=[FULL, FULL],
        out_specs=FULL,
        out_shape=jax.ShapeDtypeStruct((count * CH * owner.shape[0], LANES), jnp.float32),
        compiler_params=PARAMS,
        name="pick",
    )(owner, got)


UNIT = (4, 4, 2, 4, 8, 8, LANES)


def main_call(core, own, other, rows, coef, label):
    f32 = jnp.float32
    return pl.pallas_call(
        main_kernel,
        grid=(4,),
        in_specs=[
            pl.BlockSpec(memory_space=SMEM),
            FULL, FULL, FULL,
            FULL, FULL,
        ],
        out_specs=[
            FULL,
            FULL,
            FULL,
        ],
        out_shape=[
            jax.ShapeDtypeStruct((16, 16, LANES), f32),
            jax.ShapeDtypeStruct(UNIT, f32),
            jax.ShapeDtypeStruct((2, 8, 8, 8, LANES), f32),
        ],
        scratch_shapes=[pltpu.VMEM((2, 8, LANES), f32)],
        compiler_params=PARAMS,
        name="pairs",
    )(core, own, other, rows, coef, label)


def weigh_call(classes, core, parts, unit, own, other, sup, coef):
    f32 = jnp.float32
    return pl.pallas_call(
        functools.partial(weigh_kernel, classes),
        grid=(4,),
        in_specs=[
            pl.BlockSpec(memory_space=SMEM),
            FULL,
            FULL,
            FULL, FULL,
            FULL,
            FULL,
        ],
        out_specs=FULL,
        out_shape=jax.ShapeDtypeStruct((384, LANES), f32),
        scratch_shapes=[pltpu.VMEM((2, 16, 8, LANES), f32), pltpu.VMEM((4, 6, 8, 8, LANES), f32)],
        compiler_params=PARAMS,
        name="weigh",
    )(core, parts, unit, own, other, sup, coef)


def local(tgt_n, sup_n, targets, labels, support_slots, block_owner, dual_coeffs):
    blocks = dual_coeffs.shape[0]
    classes = dual_coeffs.shape[2]
    index = lax.axis_index("tgt")
    core = (index % 2)[None].astype(jnp.int32)
    partner = [(t, t ^ 1) for t in range(tgt_n)]
    planes = [[t for t in range(tgt_n) if t % 2 == c] for c in range(2)]
    sets = [
        [t * sup_n + s for t in (2 * k, 2 * k + 1) for s in range(sup_n)] for k in range(tgt_n // 2)
    ]
    slot = slot_call(support_slots[0].transpose(1, 0, 2)).reshape(tgt_n, 4, LANES)
    got = lax.all_to_all(slot, "tgt", 0, 0, tiled=True)
    own, coef, owner = target_call(core, block_owner, targets, dual_coeffs)
    got, own, owner = lax.optimization_barrier((got, own, owner))
    other = lax.ppermute(own, "tgt", partner)
    half_n = tgt_n // 2
    piece_shape = (half_n, CH, blocks, LANES)
    rows = lax.all_to_all(
        pick_call(owner, got, half_n).reshape(piece_shape), "tgt", 0, 0,
        axis_index_groups=planes, tiled=True,
    ).reshape(half_n * blocks * CH, LANES)
    first = lax.axis_index("sup") == 0
    label = jnp.where(first, labels.astype(jnp.float32), 0.0)[:, None]
    parts, unit, sup = main_call(core, own, other, rows, coef, label)
    parts = lax.all_to_all(
        parts, ("tgt", "sup"), 0, 0, axis_index_groups=sets, tiled=True
    )
    grad = weigh_call(classes, core, parts, unit, own, other, sup, coef)
    grad = lax.all_to_all(
        grad.reshape(piece_shape), "tgt", 0, 0, axis_index_groups=planes, tiled=True
    )
    full = fold_call(grad.reshape(half_n * blocks * CH, LANES)).reshape(piece_shape)
    full = lax.all_to_all(
        full, "tgt", 0, 0, axis_index_groups=planes, tiled=True
    )
    theirs = lax.ppermute(full, "tgt", partner)
    even = jnp.where(core[0] == 0, full, theirs)
    odd = jnp.where(core[0] == 0, theirs, full)
    both = jnp.stack([even, odd]).reshape(2, 8, 4, CH, blocks, LANES)
    out = both.transpose(4, 2, 0, 3, 1, 5).reshape(blocks, 8, CH, PIX)
    pred = jnp.sum(lax.dynamic_slice_in_dim(parts, core[0] * 8, 8, 1), axis=0)
    return pred[:, :classes], out


def solution(mesh):
    return jax.shard_map(
        functools.partial(local, mesh.shape["tgt"], mesh.shape["sup"]),
        mesh=mesh,
        in_specs=(
            P("tgt", None, None),
            P("tgt"),
            P("tgt", "sup", None, None),
            P(),
            P(None, "sup", None),
        ),
        out_specs=(P("tgt", None), P(None, "sup", None, None)),
        check_vma=False,
    )
```

```python
import functools

import jax
import jax.numpy as jnp
from jax import lax
from jax.experimental import pallas as pl
from jax.experimental.pallas import tpu as pltpu
from jax.sharding import PartitionSpec as P

LANES = 128
PIX = 1024
CH = 3
ALPHA = 1.6 / 9.0
W = 1.6
BIAS = 0.1
LOSS = 64.0
Q = 2.0 / 3.141592653589793

WIDE = (0.9999998602381658, 0.16669029577848243, 0.07435772061999424,
        0.05091170352566525, 0.0038116604731453715, 0.0690369823030177)
NARROW = (1.000000019010712, 0.16666188274704566, 0.07519150147740127, 0.04200062838628592,
          0.04465464851544397)


def half_arcsin(z, o, r, coefficients):
    y = z * lax.rsqrt(1.0 + o * r)
    y2 = y * y
    scaled = [2.0**0.5 * c * 0.5**k for k, c in enumerate(coefficients)]
    total = scaled[-1]
    for c in scaled[-2::-1]:
        total = total * y2 + c
    return y * total


def lane_masks():
    lane = lax.broadcasted_iota(jnp.int32, (8, LANES), 1)
    edges = (lane % 8 > 0, lane % 8 < 7, lane >= 8, lane < LANES - 8)
    k, h, c = lane // 16, lane // 8 % 2, lane % 8
    tiled = (2 * h + k // 4) * 32 + 4 * c + k % 4
    row, col = lane // 32, lane % 32
    natural = ((row % 2) * 4 + col % 4) * 16 + (row // 2) * 8 + col // 4
    swap = [(lane // (16 * bit)) % 2 == 1 for bit in (1, 2, 4)]
    return edges, tiled, natural, swap


def box(v, masks):
    left, right, above, below = masks[0]
    r = []
    for i in (0, 4):
        c0, c1, c2, c3 = v[i:i + 4]
        p, q = c0 + c1, c2 + c3
        r.append(p + jnp.where(left, pltpu.roll(c3, 1, 1), 0.0))
        r.append(p + c2)
        r.append(c1 + q)
        r.append(q + jnp.where(right, pltpu.roll(c0, LANES - 1, 1), 0.0))
    out = [None] * 8
    for j in range(4):
        a, b = r[j], r[4 + j]
        p = a + b
        out[j] = p + jnp.where(above, pltpu.roll(b, 8, 1), 0.0)
        out[4 + j] = p + jnp.where(below, pltpu.roll(a, LANES - 8, 1), 0.0)
    return out


def exchange_blocks(v, masks):
    v = list(v)
    for n, bit in enumerate((1, 2, 4)):
        odd = masks[3][n]
        for i in range(8):
            if not i & bit:
                a, b = v[i], v[i + bit]
                v[i] = jnp.where(odd, pltpu.roll(b, 16 * bit, 1), a)
                v[i + bit] = jnp.where(odd, b, pltpu.roll(a, LANES - 16 * bit, 1))
    return v


def interleave(nat, masks):
    return exchange_blocks([jnp.take_along_axis(a, masks[1], axis=1) for a in nat], masks)


def chain(channels, masks):
    squares = [a * a + b * b + d * d for a, b, d in zip(*channels)]
    n = [(ALPHA / CH) * a + BIAS for a in box(squares, masks)]
    factors, slopes = [], []
    for h in range(3):
        b = [lax.rsqrt(1.0 + 2.0 * a) for a in n]
        factors.append(b)
        if h < 2:
            act = []
            slope = []
            for a, bb in zip(n, b):
                inv = bb * bb
                z = 2.0 * a * inv
                rr = lax.rsqrt(1.0 + 4.0 * a)
                o = (1.0 + 4.0 * a) * (inv * inv)
                r = (1.0 + 2.0 * a) * rr
                act.append(half_arcsin(z, o, r, WIDE if h == 0 else NARROW))
                slope.append(2.0 * Q * inv * rr)
            slopes.append(slope)
            n = [(ALPHA * Q) * a + BIAS for a in box(act, masks)]
    return factors, slopes


def slot_kernel(slot_ref, out_ref):
    for ch in range(CH):
        for m in range(8):
            out_ref[pl.ds(m * 24 + ch, 8, stride=3), :] = slot_ref[ch, :, m * LANES:(m + 1) * LANES]


def target_kernel(core_ref, owner_ref, images_ref, coef_ref, out_ref, rows_ref, lanes_ref):
    masks = lane_masks()
    chans = []
    for ch in range(CH):
        nat = [images_ref[:, ch, m * LANES:(m + 1) * LANES] for m in range(8)]
        chans.append(interleave(nat, masks))
    factors, _ = chain(chans, masks)
    for r in range(8):
        for ch in range(CH):
            out_ref[ch, r] = (1.0 / (CH * Q)) * chans[ch][r]
        for h in range(3):
            out_ref[3 + h, r] = (2.0 * ALPHA * Q) * factors[h][r]
    for g in range(2):
        rows_ref[g] = coef_rows(coef_ref, core_ref[0], g)
    for b in range(owner_ref.shape[0]):
        lanes_ref[b:b + 1, :] = jnp.full((1, LANES), owner_ref[b], jnp.int32)


def coef_rows(coef_ref, core, g):
    both = []
    for b in range(2):
        rows = coef_ref[2 * g + b]
        pick = [jnp.where(core == 0, rows[2 * k:2 * k + 1], rows[2 * k + 1:2 * k + 2]) for k in range(4)]
        both.extend(pick)
    rows = jnp.concatenate(both, axis=0)
    return jnp.concatenate([rows, jnp.zeros((8, LANES - rows.shape[1]), jnp.float32)], axis=1)


def pair_chain(tgt, sup, masks, put):
    R = range(8)

    def layer(h, S, theta):
        p2 = [tgt(3 + h, r) * sup(3 + h, r) for r in R]
        z = [p * s for p, s in zip(p2, S)]
        o = [1.0 - a * a for a in z]
        rt = [lax.rsqrt(a) for a in o]
        act = [half_arcsin(a, b, c, WIDE if h == 0 else NARROW) for a, b, c in zip(z, o, rt)]
        D = [a * b for a, b in zip(p2, rt)]
        f = [a * b * (c * c) for a, b, c in zip(p2, theta, rt)]
        return z, act, rt, D, f

    cross = [tgt(0, r) * sup(0, r) + tgt(1, r) * sup(1, r) + tgt(2, r) * sup(2, r) for r in R]
    yield
    S1 = [a + BIAS / (ALPHA * Q) for a in box(cross, masks)]
    yield
    z1, A1, u1, D1, f1 = layer(0, S1, S1)
    yield
    back = box([x * y for x, y in zip(S1, D1)], masks)
    S2 = [a + BIAS / (ALPHA * Q) for a in box(A1, masks)]
    T2 = [s + a for s, a in zip(S2, back)]
    yield
    z2, A2, u2, D2, f2 = layer(1, S2, T2)
    yield
    back = box([x * y for x, y in zip(T2, D2)], masks)
    S3 = [a + BIAS / (ALPHA * Q) for a in box(A2, masks)]
    T3 = [s + a for s, a in zip(S3, back)]
    yield
    z3, A3, u3, D3, f3 = layer(2, S3, T3)
    yield
    gp = box(D3, masks)
    gs = [D3[r] * (2.0 + z3[r] * f3[r]) for r in R]
    for r in R:
        put(3, r, u3[r] * (z3[r] + f3[r]))
    ga = box(gs, masks)
    terms = [A3[r] + T3[r] * D3[r] for r in R]
    while len(terms) > 1:
        terms = [a + b for a, b in zip(terms[::2], terms[1::2])]
    entry = jnp.sum(terms[0], axis=1, keepdims=True) * (W * Q / PIX) + BIAS
    yield
    gt, gs = [], []
    for r in R:
        e = gp[r] * f2[r]
        put(2, r, u2[r] * (z2[r] * ga[r] + e))
        gt.append(gp[r] * D2[r])
        gs.append(D2[r] * (ga[r] + gp[r] + z2[r] * e))
    gp = box(gt, masks)
    ga = box(gs, masks)
    yield
    gs = []
    for r in R:
        e = gp[r] * f1[r]
        put(1, r, u1[r] * (z1[r] * ga[r] + e))
        gs.append(D1[r] * (ga[r] + gp[r] + z1[r] * e))
    gx = box(gs, masks)
    for r in R:
        put(0, r, gx[r])
    yield entry


def main_kernel(core_ref, own_ref, other_ref, rows_ref, coef_ref, label_ref,
                parts_ref, unit_ref, sup_ref, kt_ref):
    masks = lane_masks()
    core = core_ref[0]
    step = pl.program_id(0)

    @pl.when(step == 0)
    def _():
        for g in range(2):
            chans = []
            for ch in range(CH):
                nat = []
                for m in range(8):
                    pieces = [
                        rows_ref[pl.ds(m * 48 + ch * 4 + 2 * g + b, 4, stride=12), :]
                        for b in range(2)
                    ]
                    nat.append(jnp.concatenate(pieces, axis=0))
                chans.append(exchange_blocks(nat, masks))
            factors, slopes = chain(chans, masks)
            for r in range(8):
                for ch in range(CH):
                    sup_ref[g, ch, r] = chans[ch][r]
                for h in range(3):
                    sup_ref[g, 3 + h, r] = factors[h][r]
                for h in range(2):
                    sup_ref[g, 6 + h, r] = slopes[h][r]
        kt_ref[...] = jnp.zeros_like(kt_ref)

    g = step // 2
    lane = lax.broadcasted_iota(jnp.int32, (8, LANES), 1)

    def pair(i2, carry):
        def start(i, half, ref):
            t = (step % 2) * 4 + i

            def tgt(k, r):
                return jnp.broadcast_to(ref[k, r, pl.ds(t, 1), :], (8, LANES))

            def sup(k, r):
                return sup_ref[g, k, r]

            def put(k, r, value):
                unit_ref[step, i, half, k, r] = value

            return pair_chain(tgt, sup, masks, put)

        entries = None
        chains = [start(2 * i2 + j, half, ref) for j in range(2) for half, ref in enumerate((own_ref, other_ref))]
        for entries in zip(*chains):
            pass
        kt = kt_ref[g]
        for j in range(2):
            for half in range(2):
                kt = jnp.where(lane == 8 * half + (step % 2) * 4 + 2 * i2 + j, entries[2 * j + half], kt)
        kt_ref[g] = kt
        return carry

    lax.fori_loop(0, 2, pair, 0)

    @pl.when(step == 3)
    def _():
        part = None
        for g2 in range(2):
            term = lax.dot_general(
                kt_ref[g2], coef_ref[g2], (((0,), (0,)), ((), ())),
                precision=lax.Precision.HIGHEST, preferred_element_type=jnp.float32,
            )
            part = term if part is None else part + term
        own, other = part[0:8], part[8:16]
        own = jnp.where(lane == LANES - 1, label_ref[...], own)
        for peer in range(16):
            parts_ref[peer, pl.ds(pl.multiple_of(core * 8, 8), 8), :] = own
            parts_ref[peer, pl.ds(pl.multiple_of((1 - core) * 8, 8), 8), :] = other


def weigh_kernel(classes, core_ref, parts_ref, unit_ref, own_ref, other_ref, sup_ref, coef_ref,
                 grad_ref, weight_ref, acc_ref):
    masks = lane_masks()
    core = core_ref[0]
    step = pl.program_id(0)
    lane = lax.broadcasted_iota(jnp.int32, (8, LANES), 1)

    @pl.when(step == 0)
    def _():
        errs = []
        for start in (core * 8, (1 - core) * 8):
            start = pl.multiple_of(start, 8)
            vs = [parts_ref[peer, pl.ds(start, 8), :] for peer in range(16)]
            while len(vs) > 1:
                vs = [a + b for a, b in zip(vs[::2], vs[1::2])]
            v = vs[0]
            label = v[:, LANES - 1:LANES]
            onehot = jnp.where(lane.astype(jnp.float32) == label, 1.0, 0.0)
            errs.append(jnp.where(lane < classes, LOSS * (v - onehot), 0.0))
        err = jnp.concatenate(errs, axis=0)
        for g in range(2):
            wt = lax.dot_general(
                coef_ref[g], err, (((1,), (1,)), ((), ())),
                precision=lax.Precision.HIGHEST, preferred_element_type=jnp.float32,
            ) * (W * Q / PIX)
            for t in range(16):
                weight_ref[g, t] = jnp.broadcast_to(wt[:, t:t + 1], (8, LANES))

    g = step // 2
    part = step % 2
    for r in range(8):
        acc = [None] * 6
        for i in range(4):
            for half, ref in enumerate((own_ref, other_ref)):
                t = part * 4 + i
                w = weight_ref[g, half * 8 + t]
                x = w * unit_ref[step, i, half, 0, r]
                terms = [
                    x * jnp.broadcast_to(ref[ch, r, pl.ds(t, 1), :], (8, LANES)) for ch in range(CH)
                ] + [w * unit_ref[step, i, half, 1 + h, r] for h in range(3)]
                acc = [b if a is None else a + b for a, b in zip(acc, terms)]
        for k in range(6):
            acc_ref[step, k, r] = acc[k]

    @pl.when(step == 3)
    def _():
        R = range(8)

        def variance(g, h):
            return [
                -(sup_ref[g, 3 + h, r] * sup_ref[g, 3 + h, r])
                * (acc_ref[2 * g, 3 + h, r] + acc_ref[2 * g + 1, 3 + h, r])
                for r in R
            ]

        G = range(2)
        gn = [variance(g, 2) for g in G]
        for h in (1, 0):
            back = [box(gn[g], masks) for g in G]
            own = [variance(g, h) for g in G]
            gn = [[own[g][r] + ALPHA * back[g][r] * sup_ref[g, 6 + h, r] for r in R] for g in G]
        back = [box(gn[g], masks) for g in G]
        for ch in range(CH):
            for g in G:
                v = [
                    acc_ref[2 * g, ch, r] + acc_ref[2 * g + 1, ch, r]
                    + (2.0 * ALPHA / CH) * sup_ref[g, ch, r] * back[g][r]
                    for r in R
                ]
                nat = exchange_blocks(v, masks)
                for m in range(8):
                    for b in range(2):
                        grad_ref[pl.ds(m * 48 + ch * 4 + 2 * g + b, 4, stride=12), :] = nat[m][4 * b:4 * b + 4]


VMEM = pltpu.MemorySpace.VMEM
SMEM = pltpu.MemorySpace.SMEM
FULL = pl.BlockSpec(memory_space=VMEM)
PARAMS = pltpu.CompilerParams(vmem_limit_bytes=24 * 2**20)


def fold_kernel(parts_ref, out_ref):
    vs = [parts_ref[k * 24:k * 24 + 24, :] for k in range(parts_ref.shape[0] // 24)]
    while len(vs) > 1:
        vs = [a + b for a, b in zip(vs[::2], vs[1::2])]
    half = vs[0].shape[0] // 2
    piece = vs[0][:half] + vs[0][half:]
    twice = jnp.concatenate([piece, piece], axis=0)
    natural = jnp.broadcast_to(lane_masks()[2][0:1], twice.shape)
    twice = jnp.take_along_axis(twice, natural, axis=1)
    for k in range(out_ref.shape[0] // 24):
        out_ref[k * 24:k * 24 + 24, :] = twice


def fold_call(parts):
    return pl.pallas_call(
        fold_kernel,
        in_specs=[FULL], out_specs=FULL,
        out_shape=jax.ShapeDtypeStruct(parts.shape, jnp.float32),
        compiler_params=PARAMS,
        name="fold",
    )(parts)


def slot_call(slot):
    return pl.pallas_call(
        slot_kernel,
        in_specs=[FULL], out_specs=FULL,
        out_shape=jax.ShapeDtypeStruct((192, LANES), jnp.float32),
        compiler_params=PARAMS,
        name="slot",
    )(slot)


def target_call(core, owner, images, coef):
    f32 = jnp.float32
    return pl.pallas_call(
        target_kernel,
        in_specs=[pl.BlockSpec(memory_space=SMEM)] * 2 + [FULL, FULL],
        out_specs=[FULL] * 3,
        out_shape=[
            jax.ShapeDtypeStruct((6, 8, 8, LANES), f32),
            jax.ShapeDtypeStruct((2, 8, LANES), f32),
            jax.ShapeDtypeStruct((owner.shape[0], LANES), jnp.int32),
        ],
        compiler_params=PARAMS,
        name="targets",
    )(core, owner, images, coef)


def pick_kernel(owner_ref, got_ref, out_ref):
    count = owner_ref.shape[0]
    rows = 8 * CH
    place = lax.broadcasted_iota(jnp.int32, (rows, LANES), 0) // CH
    blocks = [jnp.zeros((rows, LANES), jnp.float32)] * count
    owners = [jnp.broadcast_to(owner_ref[b:b + 1, :], (rows, LANES)) - place for b in range(count)]
    for k in range(got_ref.shape[0] // rows):
        v = got_ref[k * rows:(k + 1) * rows, :]
        blocks = [jnp.where(o == 8 * k, v, a) for o, a in zip(owners, blocks)]
    sums = []
    for a in blocks:
        parts = [a[CH * k:CH * (k + 1)] for k in range(8)]
        while len(parts) > 1:
            parts = [x + y for x, y in zip(parts[::2], parts[1::2])]
        sums.append(parts[0])
    piece = [v[ch:ch + 1] for ch in range(CH) for v in sums]
    twice = jnp.concatenate(piece + piece, axis=0)
    tiled = jnp.broadcast_to(lane_masks()[1][0:1], twice.shape)
    twice = jnp.take_along_axis(twice, tiled, axis=1)
    for k in range(out_ref.shape[0] // twice.shape[0]):
        out_ref[k * twice.shape[0]:(k + 1) * twice.shape[0], :] = twice


def pick_call(owner, got, count):
    return pl.pallas_call(
        pick_kernel,
        in_specs=[FULL, FULL],
        out_specs=FULL,
        out_shape=jax.ShapeDtypeStruct((count * CH * owner.shape[0], LANES), jnp.float32),
        compiler_params=PARAMS,
        name="pick",
    )(owner, got)


UNIT = (4, 4, 2, 4, 8, 8, LANES)


def main_call(core, own, other, rows, coef, label):
    f32 = jnp.float32
    return pl.pallas_call(
        main_kernel,
        grid=(4,),
        in_specs=[
            pl.BlockSpec(memory_space=SMEM),
            FULL, FULL, FULL,
            FULL, FULL,
        ],
        out_specs=[
            FULL,
            FULL,
            FULL,
        ],
        out_shape=[
            jax.ShapeDtypeStruct((16, 16, LANES), f32),
            jax.ShapeDtypeStruct(UNIT, f32),
            jax.ShapeDtypeStruct((2, 8, 8, 8, LANES), f32),
        ],
        scratch_shapes=[pltpu.VMEM((2, 8, LANES), f32)],
        compiler_params=PARAMS,
        name="pairs",
    )(core, own, other, rows, coef, label)


def weigh_call(classes, core, parts, unit, own, other, sup, coef):
    f32 = jnp.float32
    return pl.pallas_call(
        functools.partial(weigh_kernel, classes),
        grid=(4,),
        in_specs=[
            pl.BlockSpec(memory_space=SMEM),
            FULL,
            FULL,
            FULL, FULL,
            FULL,
            FULL,
        ],
        out_specs=FULL,
        out_shape=jax.ShapeDtypeStruct((384, LANES), f32),
        scratch_shapes=[pltpu.VMEM((2, 16, 8, LANES), f32), pltpu.VMEM((4, 6, 8, 8, LANES), f32)],
        compiler_params=PARAMS,
        name="weigh",
    )(core, parts, unit, own, other, sup, coef)


def local(tgt_n, sup_n, targets, labels, support_slots, block_owner, dual_coeffs):
    blocks = dual_coeffs.shape[0]
    classes = dual_coeffs.shape[2]
    index = lax.axis_index("tgt")
    core = (index % 2)[None].astype(jnp.int32)
    partner = [(t, t ^ 1) for t in range(tgt_n)]
    planes = [[t for t in range(tgt_n) if t % 2 == c] for c in range(2)]
    sets = [
        [t * sup_n + s for t in (2 * k, 2 * k + 1) for s in range(sup_n)] for k in range(tgt_n // 2)
    ]
    slot = slot_call(support_slots[0].transpose(1, 0, 2)).reshape(tgt_n, 1, CH * LANES)
    got = lax.all_to_all(slot, "tgt", 0, 0, tiled=True)
    own, coef, owner = target_call(core, block_owner, targets, dual_coeffs)
    got, own, owner = lax.optimization_barrier((got, own, owner))
    other = lax.ppermute(own, "tgt", partner)
    half_n = tgt_n // 2
    piece_shape = (half_n, CH, blocks, LANES)
    rows = lax.all_to_all(
        pick_call(owner, got.reshape(tgt_n * CH, LANES), half_n).reshape(piece_shape), "tgt", 0, 0,
        axis_index_groups=planes, tiled=True,
    ).reshape(half_n * blocks * CH, LANES)
    first = lax.axis_index("sup") == 0
    label = jnp.where(first, labels.astype(jnp.float32), 0.0)[:, None]
    parts, unit, sup = main_call(core, own, other, rows, coef, label)
    parts = lax.all_to_all(
        parts, ("tgt", "sup"), 0, 0, axis_index_groups=sets, tiled=True
    )
    grad = weigh_call(classes, core, parts, unit, own, other, sup, coef)
    grad = lax.all_to_all(
        grad.reshape(piece_shape), "tgt", 0, 0, axis_index_groups=planes, tiled=True
    )
    full = fold_call(grad.reshape(half_n * blocks * CH, LANES)).reshape(piece_shape)
    full = lax.all_to_all(
        full, "tgt", 0, 0, axis_index_groups=planes, tiled=True
    )
    theirs = lax.ppermute(full, "tgt", partner)
    even = jnp.where(core[0] == 0, full, theirs)
    odd = jnp.where(core[0] == 0, theirs, full)
    both = jnp.stack([even, odd]).reshape(2, 8, 4, CH, blocks, LANES)
    out = both.transpose(4, 2, 0, 3, 1, 5).reshape(blocks, 8, CH, PIX)
    pred = jnp.sum(lax.dynamic_slice_in_dim(parts, core[0] * 8, 8, 1), axis=0)
    return pred[:, :classes], out


def solution(mesh):
    return jax.shard_map(
        functools.partial(local, mesh.shape["tgt"], mesh.shape["sup"]),
        mesh=mesh,
        in_specs=(
            P("tgt", None, None),
            P("tgt"),
            P("tgt", "sup", None, None),
            P(),
            P(None, "sup", None),
        ),
        out_specs=(P("tgt", None), P(None, "sup", None, None)),
        check_vma=False,
    )
```

```python
import functools

import jax
import jax.numpy as jnp
from jax import lax
from jax.experimental import pallas as pl
from jax.experimental.pallas import tpu as pltpu
from jax.sharding import PartitionSpec as P

LANES = 128
PIX = 1024
CH = 3
ALPHA = 1.6 / 9.0
W = 1.6
BIAS = 0.1
LOSS = 64.0
Q = 2.0 / 3.141592653589793

WIDE = (0.9999998602381658, 0.16669029577848243, 0.07435772061999424,
        0.05091170352566525, 0.0038116604731453715, 0.0690369823030177)
NARROW = (1.000000019010712, 0.16666188274704566, 0.07519150147740127, 0.04200062838628592,
          0.04465464851544397)


def half_arcsin(z, o, r, coefficients):
    y = z * lax.rsqrt(1.0 + o * r)
    y2 = y * y
    scaled = [2.0**0.5 * c * 0.5**k for k, c in enumerate(coefficients)]
    total = scaled[-1]
    for c in scaled[-2::-1]:
        total = total * y2 + c
    return y * total


def lane_masks():
    lane = lax.broadcasted_iota(jnp.int32, (8, LANES), 1)
    edges = (lane % 8 > 0, lane % 8 < 7, lane >= 8, lane < LANES - 8)
    k, h, c = lane // 16, lane // 8 % 2, lane % 8
    tiled = (2 * h + k // 4) * 32 + 4 * c + k % 4
    row, col = lane // 32, lane % 32
    natural = ((row % 2) * 4 + col % 4) * 16 + (row // 2) * 8 + col // 4
    swap = [(lane // (16 * bit)) % 2 == 1 for bit in (1, 2, 4)]
    return edges, tiled, natural, swap


def box(v, masks):
    left, right, above, below = masks[0]
    r = []
    for i in (0, 4):
        c0, c1, c2, c3 = v[i:i + 4]
        p, q = c0 + c1, c2 + c3
        r.append(p + jnp.where(left, pltpu.roll(c3, 1, 1), 0.0))
        r.append(p + c2)
        r.append(c1 + q)
        r.append(q + jnp.where(right, pltpu.roll(c0, LANES - 1, 1), 0.0))
    out = [None] * 8
    for j in range(4):
        a, b = r[j], r[4 + j]
        p = a + b
        out[j] = p + jnp.where(above, pltpu.roll(b, 8, 1), 0.0)
        out[4 + j] = p + jnp.where(below, pltpu.roll(a, LANES - 8, 1), 0.0)
    return out


def exchange_blocks(v, masks):
    v = list(v)
    for n, bit in enumerate((1, 2, 4)):
        odd = masks[3][n]
        for i in range(8):
            if not i & bit:
                a, b = v[i], v[i + bit]
                v[i] = jnp.where(odd, pltpu.roll(b, 16 * bit, 1), a)
                v[i + bit] = jnp.where(odd, b, pltpu.roll(a, LANES - 16 * bit, 1))
    return v


def interleave(nat, masks):
    return exchange_blocks([jnp.take_along_axis(a, masks[1], axis=1) for a in nat], masks)


def chain(channels, masks):
    squares = [a * a + b * b + d * d for a, b, d in zip(*channels)]
    n = [(ALPHA / CH) * a + BIAS for a in box(squares, masks)]
    factors, slopes = [], []
    for h in range(3):
        b = [lax.rsqrt(1.0 + 2.0 * a) for a in n]
        factors.append(b)
        if h < 2:
            act = []
            slope = []
            for a, bb in zip(n, b):
                inv = bb * bb
                z = 2.0 * a * inv
                rr = lax.rsqrt(1.0 + 4.0 * a)
                o = (1.0 + 4.0 * a) * (inv * inv)
                r = (1.0 + 2.0 * a) * rr
                act.append(half_arcsin(z, o, r, WIDE if h == 0 else NARROW))
                slope.append(2.0 * Q * inv * rr)
            slopes.append(slope)
            n = [(ALPHA * Q) * a + BIAS for a in box(act, masks)]
    return factors, slopes


def slot_kernel(slot_ref, out_ref):
    for ch in range(CH):
        for m in range(8):
            out_ref[pl.ds(m * 24 + ch, 8, stride=3), :] = slot_ref[ch, :, m * LANES:(m + 1) * LANES]


def target_kernel(core_ref, owner_ref, images_ref, coef_ref, out_ref, rows_ref, lanes_ref):
    masks = lane_masks()
    chans = []
    for ch in range(CH):
        nat = [images_ref[:, ch, m * LANES:(m + 1) * LANES] for m in range(8)]
        chans.append(interleave(nat, masks))
    factors, _ = chain(chans, masks)
    for r in range(8):
        for ch in range(CH):
            out_ref[ch, r] = (1.0 / (CH * Q)) * chans[ch][r]
        for h in range(3):
            out_ref[3 + h, r] = (2.0 * ALPHA * Q) * factors[h][r]
    for g in range(2):
        rows_ref[g] = coef_rows(coef_ref, core_ref[0], g)
    for b in range(owner_ref.shape[0]):
        lanes_ref[b:b + 1, :] = jnp.full((1, LANES), owner_ref[b], jnp.int32)


def coef_rows(coef_ref, core, g):
    both = []
    for b in range(2):
        rows = coef_ref[2 * g + b]
        pick = [jnp.where(core == 0, rows[2 * k:2 * k + 1], rows[2 * k + 1:2 * k + 2]) for k in range(4)]
        both.extend(pick)
    rows = jnp.concatenate(both, axis=0)
    return jnp.concatenate([rows, jnp.zeros((8, LANES - rows.shape[1]), jnp.float32)], axis=1)


def pair_chain(tgt, sup, masks, put):
    R = range(8)

    def layer(h, S, theta):
        p2 = [tgt(3 + h, r) * sup(3 + h, r) for r in R]
        z = [p * s for p, s in zip(p2, S)]
        o = [1.0 - a * a for a in z]
        rt = [lax.rsqrt(a) for a in o]
        act = [half_arcsin(a, b, c, WIDE if h == 0 else NARROW) for a, b, c in zip(z, o, rt)]
        D = [a * b for a, b in zip(p2, rt)]
        f = [a * b * (c * c) for a, b, c in zip(p2, theta, rt)]
        return z, act, rt, D, f

    cross = [tgt(0, r) * sup(0, r) + tgt(1, r) * sup(1, r) + tgt(2, r) * sup(2, r) for r in R]
    yield
    S1 = [a + BIAS / (ALPHA * Q) for a in box(cross, masks)]
    yield
    z1, A1, u1, D1, f1 = layer(0, S1, S1)
    yield
    back = box([x * y for x, y in zip(S1, D1)], masks)
    S2 = [a + BIAS / (ALPHA * Q) for a in box(A1, masks)]
    T2 = [s + a for s, a in zip(S2, back)]
    yield
    z2, A2, u2, D2, f2 = layer(1, S2, T2)
    yield
    back = box([x * y for x, y in zip(T2, D2)], masks)
    S3 = [a + BIAS / (ALPHA * Q) for a in box(A2, masks)]
    T3 = [s + a for s, a in zip(S3, back)]
    yield
    z3, A3, u3, D3, f3 = layer(2, S3, T3)
    yield
    gp = box(D3, masks)
    gs = [D3[r] * (2.0 + z3[r] * f3[r]) for r in R]
    for r in R:
        put(3, r, u3[r] * (z3[r] + f3[r]))
    ga = box(gs, masks)
    terms = [A3[r] + T3[r] * D3[r] for r in R]
    while len(terms) > 1:
        terms = [a + b for a, b in zip(terms[::2], terms[1::2])]
    entry = jnp.sum(terms[0], axis=1, keepdims=True) * (W * Q / PIX) + BIAS
    yield
    gt, gs = [], []
    for r in R:
        e = gp[r] * f2[r]
        put(2, r, u2[r] * (z2[r] * ga[r] + e))
        gt.append(gp[r] * D2[r])
        gs.append(D2[r] * (ga[r] + gp[r] + z2[r] * e))
    gp = box(gt, masks)
    ga = box(gs, masks)
    yield
    gs = []
    for r in R:
        e = gp[r] * f1[r]
        put(1, r, u1[r] * (z1[r] * ga[r] + e))
        gs.append(D1[r] * (ga[r] + gp[r] + z1[r] * e))
    gx = box(gs, masks)
    for r in R:
        put(0, r, gx[r])
    yield entry


def main_kernel(core_ref, own_ref, other_ref, rows_ref, coef_ref, label_ref,
                parts_ref, unit_ref, sup_ref, kt_ref):
    masks = lane_masks()
    core = core_ref[0]
    step = pl.program_id(0)

    @pl.when(step == 0)
    def _():
        for g in range(2):
            chans = []
            for ch in range(CH):
                nat = []
                for m in range(8):
                    pieces = [
                        rows_ref[pl.ds(m * 48 + ch * 4 + 2 * g + b, 4, stride=12), :]
                        for b in range(2)
                    ]
                    nat.append(jnp.concatenate(pieces, axis=0))
                chans.append(exchange_blocks(nat, masks))
            factors, slopes = chain(chans, masks)
            for r in range(8):
                for ch in range(CH):
                    sup_ref[g, ch, r] = chans[ch][r]
                for h in range(3):
                    sup_ref[g, 3 + h, r] = factors[h][r]
                for h in range(2):
                    sup_ref[g, 6 + h, r] = slopes[h][r]
        kt_ref[...] = jnp.zeros_like(kt_ref)

    g = step // 2
    lane = lax.broadcasted_iota(jnp.int32, (8, LANES), 1)

    def pair(i2, carry):
        def start(i, half, ref):
            t = (step % 2) * 4 + i

            def tgt(k, r):
                return jnp.broadcast_to(ref[k, r, pl.ds(t, 1), :], (8, LANES))

            def sup(k, r):
                return sup_ref[g, k, r]

            def put(k, r, value):
                unit_ref[step, i, half, k, r] = value

            return pair_chain(tgt, sup, masks, put)

        entries = None
        chains = [start(2 * i2 + j, half, ref) for j in range(2) for half, ref in enumerate((own_ref, other_ref))]
        for entries in zip(*chains):
            pass
        kt = kt_ref[g]
        for j in range(2):
            for half in range(2):
                kt = jnp.where(lane == 8 * half + (step % 2) * 4 + 2 * i2 + j, entries[2 * j + half], kt)
        kt_ref[g] = kt
        return carry

    lax.fori_loop(0, 2, pair, 0)

    @pl.when(step == 3)
    def _():
        part = None
        for g2 in range(2):
            term = lax.dot_general(
                kt_ref[g2], coef_ref[g2], (((0,), (0,)), ((), ())),
                precision=lax.Precision.HIGHEST, preferred_element_type=jnp.float32,
            )
            part = term if part is None else part + term
        own, other = part[0:8], part[8:16]
        own = jnp.where(lane == LANES - 1, label_ref[...], own)
        for peer in range(16):
            parts_ref[peer, pl.ds(pl.multiple_of(core * 8, 8), 8), :] = own
            parts_ref[peer, pl.ds(pl.multiple_of((1 - core) * 8, 8), 8), :] = other


def weigh_kernel(classes, core_ref, parts_ref, unit_ref, own_ref, other_ref, sup_ref, coef_ref,
                 grad_ref, weight_ref, acc_ref):
    masks = lane_masks()
    core = core_ref[0]
    step = pl.program_id(0)
    lane = lax.broadcasted_iota(jnp.int32, (8, LANES), 1)

    @pl.when(step == 0)
    def _():
        errs = []
        for start in (core * 8, (1 - core) * 8):
            start = pl.multiple_of(start, 8)
            vs = [parts_ref[peer, pl.ds(start, 8), :] for peer in range(16)]
            while len(vs) > 1:
                vs = [a + b for a, b in zip(vs[::2], vs[1::2])]
            v = vs[0]
            label = v[:, LANES - 1:LANES]
            onehot = jnp.where(lane.astype(jnp.float32) == label, 1.0, 0.0)
            errs.append(jnp.where(lane < classes, LOSS * (v - onehot), 0.0))
        err = jnp.concatenate(errs, axis=0)
        for g in range(2):
            wt = lax.dot_general(
                coef_ref[g], err, (((1,), (1,)), ((), ())),
                precision=lax.Precision.HIGHEST, preferred_element_type=jnp.float32,
            ) * (W * Q / PIX)
            for t in range(16):
                weight_ref[g, t] = jnp.broadcast_to(wt[:, t:t + 1], (8, LANES))

    g = step // 2
    part = step % 2
    for r in range(8):
        acc = [None] * 6
        for i in range(4):
            for half, ref in enumerate((own_ref, other_ref)):
                t = part * 4 + i
                w = weight_ref[g, half * 8 + t]
                x = w * unit_ref[step, i, half, 0, r]
                terms = [
                    x * jnp.broadcast_to(ref[ch, r, pl.ds(t, 1), :], (8, LANES)) for ch in range(CH)
                ] + [w * unit_ref[step, i, half, 1 + h, r] for h in range(3)]
                acc = [b if a is None else a + b for a, b in zip(acc, terms)]
        for k in range(6):
            acc_ref[step, k, r] = acc[k]

    @pl.when(step == 3)
    def _():
        R = range(8)

        def variance(g, h):
            return [
                -(sup_ref[g, 3 + h, r] * sup_ref[g, 3 + h, r])
                * (acc_ref[2 * g, 3 + h, r] + acc_ref[2 * g + 1, 3 + h, r])
                for r in R
            ]

        G = range(2)
        gn = [variance(g, 2) for g in G]
        for h in (1, 0):
            back = [box(gn[g], masks) for g in G]
            own = [variance(g, h) for g in G]
            gn = [[own[g][r] + ALPHA * back[g][r] * sup_ref[g, 6 + h, r] for r in R] for g in G]
        back = [box(gn[g], masks) for g in G]
        for ch in range(CH):
            for g in G:
                v = [
                    acc_ref[2 * g, ch, r] + acc_ref[2 * g + 1, ch, r]
                    + (2.0 * ALPHA / CH) * sup_ref[g, ch, r] * back[g][r]
                    for r in R
                ]
                nat = exchange_blocks(v, masks)
                for m in range(8):
                    for b in range(2):
                        grad_ref[pl.ds(m * 48 + ch * 4 + 2 * g + b, 4, stride=12), :] = nat[m][4 * b:4 * b + 4]


VMEM = pltpu.MemorySpace.VMEM
SMEM = pltpu.MemorySpace.SMEM
FULL = pl.BlockSpec(memory_space=VMEM)
PARAMS = pltpu.CompilerParams(vmem_limit_bytes=24 * 2**20)


def fold_kernel(parts_ref, out_ref):
    vs = [parts_ref[k * 24:k * 24 + 24, :] for k in range(parts_ref.shape[0] // 24)]
    while len(vs) > 1:
        vs = [a + b for a, b in zip(vs[::2], vs[1::2])]
    half = vs[0].shape[0] // 2
    piece = vs[0][:half] + vs[0][half:]
    twice = jnp.concatenate([piece, piece], axis=0)
    natural = jnp.broadcast_to(lane_masks()[2][0:1], twice.shape)
    twice = jnp.take_along_axis(twice, natural, axis=1)
    for k in range(out_ref.shape[0] // 24):
        out_ref[k * 24:k * 24 + 24, :] = twice


def fold_call(parts):
    return pl.pallas_call(
        fold_kernel,
        in_specs=[FULL], out_specs=FULL,
        out_shape=jax.ShapeDtypeStruct(parts.shape, jnp.float32),
        compiler_params=PARAMS,
        name="fold",
    )(parts)


def slot_call(slot):
    return pl.pallas_call(
        slot_kernel,
        grid=(1,),
        in_specs=[pl.BlockSpec(slot.shape, lambda i: (0, 0, 0))], out_specs=FULL,
        out_shape=jax.ShapeDtypeStruct((192, LANES), jnp.float32),
        compiler_params=pltpu.CompilerParams(vmem_limit_bytes=63 * 2**20),
        name="slot",
    )(slot)


def target_call(core, owner, images, coef):
    f32 = jnp.float32
    return pl.pallas_call(
        target_kernel,
        in_specs=[pl.BlockSpec(memory_space=SMEM)] * 2 + [FULL, FULL],
        out_specs=[FULL] * 3,
        out_shape=[
            jax.ShapeDtypeStruct((6, 8, 8, LANES), f32),
            jax.ShapeDtypeStruct((2, 8, LANES), f32),
            jax.ShapeDtypeStruct((owner.shape[0], LANES), jnp.int32),
        ],
        compiler_params=PARAMS,
        name="targets",
    )(core, owner, images, coef)


def pick_kernel(owner_ref, got_ref, out_ref):
    count = owner_ref.shape[0]
    rows = 8 * CH
    place = lax.broadcasted_iota(jnp.int32, (rows, LANES), 0) // CH
    blocks = [jnp.zeros((rows, LANES), jnp.float32)] * count
    owners = [jnp.broadcast_to(owner_ref[b:b + 1, :], (rows, LANES)) - place for b in range(count)]
    for k in range(got_ref.shape[0] // rows):
        v = got_ref[k * rows:(k + 1) * rows, :]
        blocks = [jnp.where(o == 8 * k, v, a) for o, a in zip(owners, blocks)]
    sums = []
    for a in blocks:
        parts = [a[CH * k:CH * (k + 1)] for k in range(8)]
        while len(parts) > 1:
            parts = [x + y for x, y in zip(parts[::2], parts[1::2])]
        sums.append(parts[0])
    piece = [v[ch:ch + 1] for ch in range(CH) for v in sums]
    twice = jnp.concatenate(piece + piece, axis=0)
    tiled = jnp.broadcast_to(lane_masks()[1][0:1], twice.shape)
    twice = jnp.take_along_axis(twice, tiled, axis=1)
    for k in range(out_ref.shape[0] // twice.shape[0]):
        out_ref[k * twice.shape[0]:(k + 1) * twice.shape[0], :] = twice


def pick_call(owner, got, count):
    return pl.pallas_call(
        pick_kernel,
        in_specs=[FULL, FULL],
        out_specs=FULL,
        out_shape=jax.ShapeDtypeStruct((count * CH * owner.shape[0], LANES), jnp.float32),
        compiler_params=PARAMS,
        name="pick",
    )(owner, got)


UNIT = (4, 4, 2, 4, 8, 8, LANES)


def main_call(core, own, other, rows, coef, label):
    f32 = jnp.float32
    return pl.pallas_call(
        main_kernel,
        grid=(4,),
        in_specs=[
            pl.BlockSpec(memory_space=SMEM),
            FULL, FULL, FULL,
            FULL, FULL,
        ],
        out_specs=[
            FULL,
            FULL,
            FULL,
        ],
        out_shape=[
            jax.ShapeDtypeStruct((16, 16, LANES), f32),
            jax.ShapeDtypeStruct(UNIT, f32),
            jax.ShapeDtypeStruct((2, 8, 8, 8, LANES), f32),
        ],
        scratch_shapes=[pltpu.VMEM((2, 8, LANES), f32)],
        compiler_params=PARAMS,
        name="pairs",
    )(core, own, other, rows, coef, label)


def weigh_call(classes, core, parts, unit, own, other, sup, coef):
    f32 = jnp.float32
    return pl.pallas_call(
        functools.partial(weigh_kernel, classes),
        grid=(4,),
        in_specs=[
            pl.BlockSpec(memory_space=SMEM),
            FULL,
            FULL,
            FULL, FULL,
            FULL,
            FULL,
        ],
        out_specs=FULL,
        out_shape=jax.ShapeDtypeStruct((384, LANES), f32),
        scratch_shapes=[pltpu.VMEM((2, 16, 8, LANES), f32), pltpu.VMEM((4, 6, 8, 8, LANES), f32)],
        compiler_params=PARAMS,
        name="weigh",
    )(core, parts, unit, own, other, sup, coef)


def local(tgt_n, sup_n, targets, labels, support_slots, block_owner, dual_coeffs):
    blocks = dual_coeffs.shape[0]
    classes = dual_coeffs.shape[2]
    index = lax.axis_index("tgt")
    core = (index % 2)[None].astype(jnp.int32)
    partner = [(t, t ^ 1) for t in range(tgt_n)]
    planes = [[t for t in range(tgt_n) if t % 2 == c] for c in range(2)]
    sets = [
        [t * sup_n + s for t in (2 * k, 2 * k + 1) for s in range(sup_n)] for k in range(tgt_n // 2)
    ]
    slot = slot_call(support_slots[0].transpose(1, 0, 2)).reshape(tgt_n, 1, CH * LANES)
    got = lax.all_to_all(slot, "tgt", 0, 0, tiled=True)
    own, coef, owner = target_call(core, block_owner, targets, dual_coeffs)
    got, own, owner = lax.optimization_barrier((got, own, owner))
    other = lax.ppermute(own, "tgt", partner)
    half_n = tgt_n // 2
    piece_shape = (half_n, CH, blocks, LANES)
    rows = lax.all_to_all(
        pick_call(owner, got.reshape(tgt_n * CH, LANES), half_n).reshape(piece_shape), "tgt", 0, 0,
        axis_index_groups=planes, tiled=True,
    ).reshape(half_n * blocks * CH, LANES)
    first = lax.axis_index("sup") == 0
    label = jnp.where(first, labels.astype(jnp.float32), 0.0)[:, None]
    parts, unit, sup = main_call(core, own, other, rows, coef, label)
    parts = lax.all_to_all(
        parts, ("tgt", "sup"), 0, 0, axis_index_groups=sets, tiled=True
    )
    grad = weigh_call(classes, core, parts, unit, own, other, sup, coef)
    grad = lax.all_to_all(
        grad.reshape(piece_shape), "tgt", 0, 0, axis_index_groups=planes, tiled=True
    )
    full = fold_call(grad.reshape(half_n * blocks * CH, LANES)).reshape(piece_shape)
    full = lax.all_to_all(
        full, "tgt", 0, 0, axis_index_groups=planes, tiled=True
    )
    theirs = lax.ppermute(full, "tgt", partner)
    even = jnp.where(core[0] == 0, full, theirs)
    odd = jnp.where(core[0] == 0, theirs, full)
    both = jnp.stack([even, odd]).reshape(2, 8, 4, CH, blocks, LANES)
    out = both.transpose(4, 2, 0, 3, 1, 5).reshape(blocks, 8, CH, PIX)
    pred = jnp.sum(lax.dynamic_slice_in_dim(parts, core[0] * 8, 8, 1), axis=0)
    return pred[:, :classes], out


def solution(mesh):
    return jax.shard_map(
        functools.partial(local, mesh.shape["tgt"], mesh.shape["sup"]),
        mesh=mesh,
        in_specs=(
            P("tgt", None, None),
            P("tgt"),
            P("tgt", "sup", None, None),
            P(),
            P(None, "sup", None),
        ),
        out_specs=(P("tgt", None), P(None, "sup", None, None)),
        check_vma=False,
    )
```
